32 devices in a mesh: dom: 16 (over z, y, x), rep: 2 (over core).
Axes of the slice: x: 2, y: 2, z: 4, core: 2. Of those that a mesh axis runs over, the one named last changes fastest.
Arguments:
- features: float32 [4, 32768, 100], P('rep', 'dom'), may hold values from -6 to 6
- neighbors: int32 [4, 32768, 16], P('rep', 'dom'), may hold values from 0 to 2175, as said below
- nbr_mask: int32 [4, 32768, 16], P('rep', 'dom'), may hold values 0 or 1
- send_rows: int32 [4, 256, 8], P('rep', 'dom'), may hold values from 0 to 2047
- halo_count: int32 [4, 256], P('rep', 'dom'), may hold values from 1 to 8, as said below
- pos_edges: int32 [4, 4096, 2], P('rep', 'dom'), may hold values from 0 to 2175, as said below
- neg_edges: int32 [4, 4096, 2], P('rep', 'dom'), may hold values from 0 to 2175, as said below
- w_one: float32 [100, 2048], P(None, ('dom', 'rep')), may hold values from -0.625 to 0.625
- b_one: float32 [2048], P(('dom', 'rep')), may hold values from -3 to 3
- w_two: float32 [2048, 47], P(('dom', 'rep')), may hold values from -0.125 to 0.125
- b_two: float32 [47], replicated, may hold values from -2 to 2
- w_one_row: float32 [100], replicated, may hold values from 2.1362305e-06 to 8.544922e-06
- w_one_col: float32 [2048], P(('dom', 'rep')), may hold values from 1.0375977e-07 to 4.1503907e-07
- w_two_row: float32 [2048], P(('dom', 'rep')), may hold values from 1.2207031e-05 to 4.8828126e-05
- w_two_col: float32 [47], replicated, may hold values from 0.0005493164 to 0.0021972656
- b_one_second: float32 [2048], P(('dom', 'rep')), may hold values from 3.051758e-08 to 1.2207032e-07
- b_two_second: float32 [47], replicated, may hold values from 1.0986328e-06 to 4.394531e-06
Outputs:
- loss: float32 [], replicated
- w_one_grad: float32 [100, 2048], P(None, ('dom', 'rep'))
- w_one_new: float32 [100, 2048], P(None, ('dom', 'rep'))
- w_one_row_new: float32 [100], replicated
- w_one_col_new: float32 [2048], P(('dom', 'rep'))
- w_two_grad: float32 [2048, 47], P(('dom', 'rep'))
- w_two_new: float32 [2048, 47], P(('dom', 'rep'))
- w_two_row_new: float32 [2048], P(('dom', 'rep'))
- w_two_col_new: float32 [47], replicated
- b_one_grad: float32 [2048], P(('dom', 'rep'))
- b_one_new: float32 [2048], P(('dom', 'rep'))
- b_one_second_new: float32 [2048], P(('dom', 'rep'))
- b_two_grad: float32 [47], replicated
- b_two_new: float32 [47], replicated
- b_two_second_new: float32 [47], replicated
The draws below stay inside these ranges and needn't reach their ends.
Inputs may be any that keep to these rules, and one draw needn't show every extreme that they name: `halo_count`: A halo slot index 2048 + s * 8 + j is only used where j is below the count of partition s to this partition; in every micro-batch one reader gets 8 rows from every partition. `neighbors`: indices below 2048 are local nodes, others halo slots. `pos_edges`: the first entry is a local node; the second as in neighbors. `neg_edges`: as pos_edges.
All inputs are finite; a program needn't handle non-finite values. No bound on the sum of `nbr_mask` on one device may be relied on, other than what follows from the above.
Results may differ from the reference program's by a relative error of at most 0.00085.
Values sent between devices are 32-bit elements; how exact they have to be, the bound alone decides.
No kernel may reach another device: no remote copies, remote signals or barrier semaphores. Data moves between devices by JAX's collectives and lax.ppermute only.
A program may use at most 128 MiB of HBM per device.

```python
import math
import jax
import jax.numpy as jnp
from jax import lax

F = 100
H = 2048
C = 47
NODE_DEV = 2048
EDGE_DEV = 256
DEG = 16
HCAP = 8
STEP = 20
PEERS = 16
MB = 4
NODES = 32768
TOTAL_EDGES = 16384
SLOTS = 128


def halo_counts(key):
    base = jax.random.fold_in(key, 11)
    counts = jax.random.randint(base, (MB, PEERS, PEERS), 1, HCAP + 1)
    chosen = jax.random.randint(jax.random.fold_in(base, 1), (MB,), 0, PEERS)
    full = jnp.arange(PEERS)[None, None, :] == chosen[:, None, None]
    return jnp.where(full, HCAP, counts).astype(jnp.int32)


def pointers(key, counts, length):
    shape = (MB, PEERS, length)
    local_pick = jax.random.randint(jax.random.fold_in(key, 1), shape, 0, NODE_DEV)
    source = jax.random.randint(jax.random.fold_in(key, 2), shape, 0, PEERS)
    reader = jnp.broadcast_to(jnp.arange(PEERS)[None, :, None], shape)
    flat = counts.reshape(MB, PEERS * PEERS)
    spots = (source * PEERS + reader).reshape(MB, PEERS * length)
    avail = jnp.take_along_axis(flat, spots, axis=1).reshape(shape)
    offset = jax.random.randint(jax.random.fold_in(key, 3), shape, 0, 1 << 20) % avail
    remote = NODE_DEV + source * HCAP + offset
    which = jax.random.randint(jax.random.fold_in(key, 4), shape, 0, 10) < 3
    return jnp.where(which, remote, local_pick).astype(jnp.int32)


def draw_halo_count(key, part):
    return halo_counts(key).reshape(MB, PEERS * PEERS)


def draw_neighbors(key, part):
    counts = halo_counts(key)
    return pointers(jax.random.fold_in(key, 21), counts, NODE_DEV * DEG).reshape(MB, PEERS * NODE_DEV, DEG)


def edge_list(key, salt):
    counts = halo_counts(key)
    ends = pointers(jax.random.fold_in(key, salt), counts, EDGE_DEV)
    starts = jax.random.randint(jax.random.fold_in(key, salt + 1), (MB, PEERS, EDGE_DEV), 0, NODE_DEV)
    return jnp.stack([starts.astype(jnp.int32), ends], axis=-1).reshape(MB, PEERS * EDGE_DEV, 2)


def draw_pos_edges(key, part):
    return edge_list(key, 31)


def draw_neg_edges(key, part):
    return edge_list(key, 41)


def with_ends(entries, key, low, high):
    longest = entries.shape.index(max(entries.shape))
    spots = []
    for shift in (0, 1):
        where = [jax.random.randint(jax.random.fold_in(key, axis), (), 0, length) for axis, length in enumerate(entries.shape)]
        where[longest] = (where[longest] + shift) % entries.shape[longest]
        spots.append(tuple(where))
    return entries.at[spots[0]].set(low).at[spots[1]].set(high)


def level_of(stream_key, extent, shards, smallest, largest):
    def one(position, shards_of):
        steps = jax.random.uniform(jax.random.fold_in(jax.random.fold_in(stream_key, 6), position), (shards_of,), jnp.float32, smallest / len(shards), largest / len(shards))
        return jnp.repeat(jnp.exp(steps), extent[position] // shards_of).reshape((-1,) + (1,) * (len(extent) - position - 1))

    level = one(*shards[0])
    for cut in shards[1:]:
        level = level * one(*cut)
    return level


def normal_values(stream_key, extent, scale, limit, split=(), dtype=jnp.bfloat16):
    entries = jax.random.normal(stream_key, extent, jnp.float32) * scale
    if len(split) > 0:
        entries = level_of(stream_key, extent, split, -0.22, 0.18) * entries
    return jnp.clip(entries, min=-limit, max=limit).astype(dtype)


def setup_inputs(seed: int = 0) -> dict:
    splits = jax.random.split(jax.random.key(seed), 18)
    return {
        "features": normal_values(splits[0], (MB, NODES, F), 1.0, 6.0, ((0, 2), (1, 16)), jnp.float32),
        "neighbors": draw_neighbors(jax.random.fold_in(splits[17], 71), 0),
        "nbr_mask": with_ends((jax.random.randint(splits[2], (MB, NODES, DEG), 0, 4) < 3).astype(jnp.int32), jax.random.fold_in(splits[2], 1), 0, 1),
        "send_rows": with_ends(jax.random.randint(splits[3], (MB, PEERS * PEERS, HCAP), 0, NODE_DEV), jax.random.fold_in(splits[3], 1), 0, NODE_DEV - 1).astype(jnp.int32),
        "halo_count": draw_halo_count(jax.random.fold_in(splits[17], 71), 0),
        "pos_edges": draw_pos_edges(jax.random.fold_in(splits[17], 71), 0),
        "neg_edges": draw_neg_edges(jax.random.fold_in(splits[17], 71), 0),
        "w_one": normal_values(splits[7], (F, H), F ** -0.5, 0.625, ((1, 32),), jnp.float32),
        "b_one": normal_values(splits[8], (H,), 0.5, 3.0, ((0, 32),), jnp.float32),
        "w_two": normal_values(splits[9], (H, C), H ** -0.5, 0.125, ((0, 32),), jnp.float32),
        "b_two": normal_values(splits[10], (C,), 0.3, 2.0, (), jnp.float32),
        "w_one_row": jnp.clip(jnp.exp(jax.random.uniform(splits[11], (F,), jnp.float32, math.log(2.136230477844947e-06), math.log(8.544921911379788e-06))), 2.136230477844947e-06, 8.544921911379788e-06),
        "w_one_col": jnp.clip(jnp.exp(math.log(4.1503906800244295e-07) - 1.3862944 * jax.random.uniform(splits[12], (H,), jnp.float32) ** level_of(splits[12], (H,), ((0, 32),), -0.2, 0.2)), 1.0375976700061074e-07, 4.1503906800244295e-07),
        "w_two_row": jnp.clip(jnp.exp(math.log(4.882812572759576e-05) - 1.3862944 * jax.random.uniform(splits[13], (H,), jnp.float32) ** level_of(splits[13], (H,), ((0, 32),), -0.2, 0.2)), 1.220703143189894e-05, 4.882812572759576e-05),
        "w_two_col": jnp.clip(jnp.exp(jax.random.uniform(splits[14], (C,), jnp.float32, math.log(0.0005493164), math.log(0.0021972656))), 0.0005493164, 0.0021972656),
        "b_one_second": jnp.clip(jnp.exp(math.log(1.2207031829802872e-07) - 1.3862944 * jax.random.uniform(splits[15], (H,), jnp.float32) ** level_of(splits[15], (H,), ((0, 32),), -0.2, 0.2)), 3.051757957450718e-08, 1.2207031829802872e-07),
        "b_two_second": jnp.clip(jnp.exp(jax.random.uniform(splits[16], (C,), jnp.float32, math.log(1.0986327652062755e-06), math.log(4.394531060825102e-06))), 1.0986327652062755e-06, 4.394531060825102e-06),
    }


@jax.custom_vjp
def low(v):
    return lax.optimization_barrier(v.astype(jnp.bfloat16)).astype(jnp.float32)

@jax.custom_vjp
def low_back(v):
    return v

def low_keep(v):
    return (low(v), None)

def low_pass(kept, grad):
    return (grad,)

def back_keep(v):
    return (v, None)

def back_low(kept, grad):
    return (low(grad),)
low.defvjp(low_keep, low_pass)
low_back.defvjp(back_keep, back_low)
tiny_eps = 1e-30
scale_eps = 0.001
clip_limit = 1.0
step_rate = 0.3
highest = lax.Precision.HIGHEST

def take_rows(table, index):
    return table[index]

def forward(w_one, b_one, w_two, b_two, features, neighbors, nbr_mask, send_rows, halo_count, pos_edges, neg_edges):
    total = jnp.float32(0.0)
    for micro in range(MB):
        send = send_rows[micro].reshape(PEERS, PEERS, HCAP)
        count = halo_count[micro].reshape(PEERS, PEERS)
        valid = (jnp.arange(HCAP)[None, None, :] < count[:, :, None]).astype(jnp.float32)

        def extend(values):
            sent = jax.vmap(take_rows)(values, send) * valid[..., None]
            taken = jnp.transpose(sent, (1, 0, 2, 3)).reshape(PEERS, SLOTS, values.shape[-1])
            return jnp.concatenate([values, taken], axis=1)
        inputs = features[micro].reshape(PEERS, NODE_DEV, F)
        buffer_x = extend(inputs)
        nbr = neighbors[micro].reshape(PEERS, NODE_DEV, DEG)
        weight_mask = nbr_mask[micro].reshape(PEERS, NODE_DEV, DEG).astype(jnp.float32)
        picked = jax.vmap(take_rows)(buffer_x, nbr)
        summed = lax.optimization_barrier(jnp.sum(picked * weight_mask[..., None], axis=2))
        degree = 1.0 + lax.optimization_barrier(jnp.sum(weight_mask, axis=2))
        agg = (inputs + summed) / degree[..., None]
        pre = jnp.einsum('pnf,fh->pnh', agg, w_one, precision=highest) + b_one
        hidden = jnp.maximum(pre, 0.0)
        outputs = jnp.einsum('pnh,hc->pnc', hidden, w_two, precision=highest) + b_two
        buffer_z = extend(outputs)
        for edges, sign in ((pos_edges, -1.0), (neg_edges, 1.0)):
            ends = edges[micro].reshape(PEERS, EDGE_DEV, 2)
            start_rows = jax.vmap(take_rows)(outputs, ends[..., 0])
            end_rows = jax.vmap(take_rows)(buffer_z, ends[..., 1])
            score = lax.optimization_barrier(jnp.sum(start_rows * end_rows, axis=-1))
            total = total + jnp.sum(jax.nn.softplus(sign * score))
    return total / (2.0 * TOTAL_EDGES)

def factored(weight, grad, row_old, col_old, decay):
    row_new = decay * row_old + (1.0 - decay) * lax.optimization_barrier(jnp.sum(grad * grad + tiny_eps, axis=1))
    col_new = decay * col_old + (1.0 - decay) * lax.optimization_barrier(jnp.sum(grad * grad + tiny_eps, axis=0))
    second = jnp.outer(row_new, col_new) / jnp.sum(row_new)
    update = grad * lax.rsqrt(second)
    update = update / jnp.maximum(1.0, jnp.sqrt(jnp.mean(update * update)) / clip_limit)
    scale = jnp.maximum(scale_eps, jnp.sqrt(jnp.mean(weight * weight)))
    return (weight - step_rate * scale * update, row_new, col_new)

def unfactored(weight, grad, second_old, decay):
    second_new = decay * second_old + (1.0 - decay) * (grad * grad + tiny_eps)
    update = grad * lax.rsqrt(second_new)
    update = update / jnp.maximum(1.0, jnp.sqrt(jnp.mean(update * update)) / clip_limit)
    scale = jnp.maximum(scale_eps, jnp.sqrt(jnp.mean(weight * weight)))
    return (weight - step_rate * scale * update, second_new)

def reference(features, neighbors, nbr_mask, send_rows, halo_count, pos_edges, neg_edges, w_one, b_one, w_two, b_two, w_one_row, w_one_col, w_two_row, w_two_col, b_one_second, b_two_second):

    def loss_of(first, first_bias, second, second_bias):
        return forward(first, first_bias, second, second_bias, features, neighbors, nbr_mask, send_rows, halo_count, pos_edges, neg_edges)
    loss, pullback = jax.vjp(loss_of, w_one, b_one, w_two, b_two)
    g_one, gb_one, g_two, gb_two = pullback(jnp.float32(1.0))
    decay = 1.0 - jnp.float32(STEP) ** (-0.8)
    w_one_new, row_one, col_one = factored(w_one, g_one, w_one_row, w_one_col, decay)
    w_two_new, row_two, col_two = factored(w_two, g_two, w_two_row, w_two_col, decay)
    b_one_new, second_one = unfactored(b_one, gb_one, b_one_second, decay)
    b_two_new, second_two = unfactored(b_two, gb_two, b_two_second, decay)
    return (loss, g_one, w_one_new, row_one, col_one, g_two, w_two_new, row_two, col_two, gb_one, b_one_new, second_one, gb_two, b_two_new, second_two)
```

```python
import jax
import jax.numpy as jnp
from jax import lax
from jax.experimental import pallas as pl
from jax.experimental.pallas import tpu as pltpu
from jax.sharding import PartitionSpec as P

F = 100
HCAP = 8
STEP = 20
LANES = 128
HALF = 64
GROUP = 16
NODE_BLOCK = 256
HID_BLOCK = 256
COL_BLOCK = 512

tiny_eps = 1e-30
scale_eps = 0.001
clip_limit = 1.0
step_rate = 0.3
f32 = jnp.float32
bf16 = jnp.bfloat16


def dot(a, b, dims=((1,), (0,))):
    return lax.dot_general(a, b, (dims, ((), ())), preferred_element_type=f32)


def split(x):
    hi = x.astype(bf16)
    lo = (x - hi.astype(f32)).astype(bf16)
    return hi, lo


def iota(shape, dim):
    return lax.broadcasted_iota(jnp.int32, shape, dim)


def one_hot(cond):
    return jnp.where(cond, 1.0, 0.0).astype(bf16)


def local_sum_kernel(idx_ref, mask_ref, x_ref, sum_ref, halo_ref, xcat, counts):
    rows = x_ref.shape[1]
    blk = pl.program_id(1)
    high = counts.shape[1] // LANES

    @pl.when(blk == 0)
    def _():
        hi, lo = split(x_ref[0])
        xcat[:, :LANES] = hi
        xcat[:, LANES:] = lo

    width = idx_ref.shape[2]
    lane = iota((1, width), 1)
    key_rows = iota((high * GROUP, width), 0)
    low_rows = iota((LANES, width), 0)
    for g in range(idx_ref.shape[1]):
        v = idx_ref[0, g : g + 1, :]
        key = jnp.where(mask_ref[0, g : g + 1, :] > 0, (v >> 7) * GROUP + lane // GROUP, -1)
        left = one_hot(key_rows == key)
        right = one_hot(low_rows == (v & (LANES - 1)))
        found = dot(left, right, ((1,), (1,))).astype(bf16)
        for h in range(high):
            counts[g * GROUP : (g + 1) * GROUP, h * LANES : (h + 1) * LANES] = found[
                h * GROUP : (h + 1) * GROUP
            ]
    both = dot(counts[:, :rows], xcat[...])
    own = x_ref[0, pl.ds(pl.multiple_of(blk * NODE_BLOCK, NODE_BLOCK), NODE_BLOCK), :]
    sum_ref[0] = both[:, :LANES] + both[:, LANES:] + own
    halo_ref[0] = counts[:, rows:]


def local_sums(idx, mask, x, slots):
    micros, rows, _ = x.shape
    groups = NODE_BLOCK // GROUP
    width = idx.shape[2]
    return pl.pallas_call(
        local_sum_kernel,
        grid=(micros, rows // NODE_BLOCK),
        in_specs=[
            pl.BlockSpec((1, groups, width), lambda m, b: (m, b, 0)),
            pl.BlockSpec((1, groups, width), lambda m, b: (m, b, 0)),
            pl.BlockSpec((1, rows, LANES), lambda m, b: (m, 0, 0)),
        ],
        out_specs=[
            pl.BlockSpec((1, NODE_BLOCK, LANES), lambda m, b: (m, b, 0)),
            pl.BlockSpec((1, NODE_BLOCK, slots), lambda m, b: (m, b, 0)),
        ],
        out_shape=[
            jax.ShapeDtypeStruct((micros, rows, LANES), f32),
            jax.ShapeDtypeStruct((micros, rows, slots), bf16),
        ],
        scratch_shapes=[
            pltpu.VMEM((rows, 2 * LANES), bf16),
            pltpu.VMEM((NODE_BLOCK, rows + slots), bf16),
        ],
        name="local_sums",
    )(idx, mask, x)


def finish_kernel(sum_ref, halo_ref, arrived_ref, agg_ref):
    slots = halo_ref.shape[2]
    arrived = arrived_ref[...].reshape(slots, LANES)
    arrived = jnp.where(iota(arrived.shape, 1) == F, 1.0, arrived)
    hi, lo = split(arrived)
    counts = halo_ref[0]
    total = sum_ref[0] + dot(counts, hi) + dot(counts, lo)
    agg = total / total[:, F : F + 1]
    agg_ref[0] = jnp.where(iota(agg.shape, 1) == F, 1.0, agg)


def finish(sums, halo, arrived):
    micros, rows, slots = halo.shape
    peers = arrived.shape[0]
    block = rows // 2
    return pl.pallas_call(
        finish_kernel,
        grid=(micros, 2),
        in_specs=[
            pl.BlockSpec((1, block, LANES), lambda m, b: (m, b, 0)),
            pl.BlockSpec((1, block, slots), lambda m, b: (m, b, 0)),
            pl.BlockSpec((peers, 1, HCAP, LANES), lambda m, b: (0, m, 0, 0)),
        ],
        out_specs=pl.BlockSpec((1, block, LANES), lambda m, b: (m, b, 0)),
        out_shape=jax.ShapeDtypeStruct((micros, rows, LANES), f32),
        name="finish",
    )(sums, halo, arrived)


def pick_kernel(ends_ref, agg_ref, out_ref, cat):
    @pl.when(pl.program_id(1) == 0)
    def _():
        hi, lo = split(agg_ref[0])
        cat[:, :LANES] = hi
        cat[:, LANES:] = lo

    rows = agg_ref.shape[1]
    ends = ends_ref[0, 0]
    which = one_hot(iota((ends.shape[0], rows), 1) == ends)
    both = dot(which, cat[...])
    out_ref[0, 0] = both[:, :LANES] + both[:, LANES:]


def pick(ends, agg):
    micros, sides, count, _ = ends.shape
    rows = agg.shape[1]
    return pl.pallas_call(
        pick_kernel,
        grid=(micros, sides),
        in_specs=[
            pl.BlockSpec((1, 1, count, 1), lambda m, s: (m, s, 0, 0)),
            pl.BlockSpec((1, rows, LANES), lambda m, s: (m, 0, 0)),
        ],
        out_specs=pl.BlockSpec((1, 1, count, LANES), lambda m, s: (m, s, 0, 0)),
        out_shape=jax.ShapeDtypeStruct((micros, sides, count, LANES), f32),
        scratch_shapes=[pltpu.VMEM((rows, 2 * LANES), bf16)],
        name="pick",
    )(ends, agg)


def first_block(ref, start, shards, hs):
    return ref[pl.ds(start, shards), 0:hs, :].reshape(shards * hs, LANES)


def head_block(ref, start, shards, hs):
    if hs % GROUP:
        return ref[pl.ds(start, shards), hs : 2 * hs, :].reshape(shards * hs, LANES)
    half = hs // 2
    packed = ref[pl.ds(start, shards), hs : hs + half, :].reshape(shards * half, LANES)
    low = iota(packed.shape, 1) < HALF
    left = jnp.where(low, packed, 0.0).reshape(shards, half, LANES)
    right = jnp.where(low, pltpu.roll(packed, HALF, 1), 0.0).reshape(shards, half, LANES)
    return jnp.concatenate([left, right], axis=1).reshape(shards * hs, LANES)


def head_terms(block):
    hi = block.astype(bf16)
    rest = block - hi.astype(f32)
    return hi, (hi.astype(f32) + pltpu.roll(rest, HALF, 1)).astype(bf16)


def layers_kernel(
    part_ref, halo_ref, arrived_ref, mine_ref, other_ref, head_bias_ref,
    grad_mine_ref, grad_other_ref, stats_ref,
    agg_row, agg_col, hidden, out_col, dz_col, dz_row,
    *, hs, slope_scale,
):
    micros, sides, count, _ = part_ref.shape
    ends = micros * sides * count
    slots = arrived_ref.shape[0] * HCAP
    shards = HID_BLOCK // hs
    blocks = mine_ref.shape[0] // shards
    low_lanes = iota((ends, LANES), 1) < HALF

    for m in range(micros):
        arrived = arrived_ref[:, m].reshape(slots, LANES)
        hi, lo = split(arrived)
        which = one_hot(iota((count, slots), 1) == halo_ref[m])
        far = dot(which, hi) + dot(which, lo)
        for s in range(sides):
            rows = part_ref[m, s]
            if s == 1:
                rows = rows + far
            at = (m * sides + s) * count
            hi, lo = split(rows)
            agg_row[at : at + count, :LANES] = hi
            agg_row[at : at + count, LANES:] = lo
            turned = rows.T
            hi, lo = split(turned)
            agg_col[:LANES, at : at + count] = hi
            agg_col[LANES:, at : at + count] = lo

    out_col[...] = jnp.zeros(out_col.shape, f32)

    for side, ref in enumerate((mine_ref, other_ref)):

        def forward(c, carry, ref=ref, side=side):
            first = first_block(ref, c * shards, shards, hs)
            hi, lo = split(first)
            both = jnp.concatenate([hi, lo], axis=1)
            head_hi, head_both = head_terms(head_block(ref, c * shards, shards, hs))
            head = jnp.concatenate([head_both, head_hi], axis=0)
            slot = side * blocks + c
            for n in range(0, ends, COL_BLOCK):
                cols = slice(n, n + COL_BLOCK)
                upper = agg_col[:LANES, cols]
                pre = dot(both, jnp.concatenate([upper, upper], axis=0))
                pre = pre + dot(hi, agg_col[LANES:, cols])
                act_hi, act_lo = split(jnp.maximum(pre, 0.0))
                hidden[slot, :HID_BLOCK, cols] = act_hi
                hidden[slot, HID_BLOCK:, cols] = act_lo
                act = jnp.concatenate([act_hi, act_lo], axis=0)
                out_col[:, cols] += dot(head, act, ((0,), (0,)))
            return carry

        lax.fori_loop(0, blocks, forward, 0)

    bias = head_bias_ref[...]
    loss = jnp.zeros((1, 1), f32)
    head_grad = jnp.zeros((HALF, 1), f32)
    sign = jnp.where(iota((1, count), 1) < count // 2, -1.0, 1.0)
    for m in range(micros):
        at = m * sides * count
        mid = at + count
        end = mid + count
        z_u = out_col[:HALF, at:mid] + out_col[HALF:, at:mid] + bias
        z_v = out_col[:HALF, mid:end] + out_col[HALF:, mid:end] + bias
        score = jnp.sum(z_u * z_v, axis=0, keepdims=True) * sign
        tail = jnp.exp(-jnp.abs(score))
        plus = jnp.maximum(score, 0.0) + jnp.log1p(tail)
        loss = loss + jnp.sum(plus, axis=1, keepdims=True)
        slope = sign * jax.nn.sigmoid(score) * slope_scale
        for start, grad in ((at, slope * z_v), (mid, slope * z_u)):
            stop = start + count
            head_grad = head_grad + jnp.sum(grad, axis=1, keepdims=True)
            hi, lo = split(grad)
            dz_col[:HALF, start:stop] = hi
            dz_col[HALF : 2 * HALF, start:stop] = hi
            dz_col[2 * HALF : 3 * HALF, start:stop] = lo
            dz_col[3 * HALF :, start:stop] = jnp.zeros((HALF, count), bf16)
            both = jnp.concatenate([hi.astype(f32), lo.astype(f32)], axis=0)
            dz_row[start:stop] = both.T.astype(bf16)
    stats_ref[:HALF] = jnp.broadcast_to(head_grad, (HALF, LANES))
    stats_ref[HALF:] = jnp.broadcast_to(loss, (8, LANES))

    for side, (ref, grad_ref) in enumerate(((mine_ref, grad_mine_ref), (other_ref, grad_other_ref))):

        def backward(c, carry, ref=ref, grad_ref=grad_ref, side=side):
            head_hi, head_both = head_terms(head_block(ref, c * shards, shards, hs))
            head = jnp.concatenate([head_both, head_hi], axis=1)
            slot = side * blocks + c
            head_sum = jnp.zeros((HID_BLOCK, LANES), f32)
            first_sum = jnp.zeros((HID_BLOCK, LANES), f32)
            for n in range(0, ends, COL_BLOCK):
                cols = slice(n, n + COL_BLOCK)
                act_hi = hidden[slot, :HID_BLOCK, cols]
                act_lo = hidden[slot, HID_BLOCK:, cols]
                grad = dot(head, dz_col[:, cols])
                grad = jnp.where(act_hi.astype(f32) > 0.0, grad, 0.0)
                hi, lo = split(grad)
                head_sum = head_sum + dot(act_hi, dz_row[cols]) + dot(act_lo, dz_row[cols])
                both = dot(hi, agg_row[cols])
                first_sum = first_sum + both[:, :LANES] + both[:, LANES:]
                first_sum = first_sum + dot(lo, agg_row[cols, :LANES])
            grad_ref[pl.ds(c * shards, shards), 0:hs, :] = first_sum.reshape(shards, hs, LANES)
            folded = (head_sum + pltpu.roll(head_sum, HALF, 1)).reshape(shards, hs, LANES)
            if hs % GROUP:
                grad_ref[pl.ds(c * shards, shards), hs : 2 * hs, :] = folded
            else:
                half = hs // 2
                low = iota((shards, half, LANES), 2) < HALF
                grad_ref[pl.ds(c * shards, shards), hs : hs + half, :] = jnp.where(
                    low, folded[:, :half], folded[:, half:]
                )
            return carry

        lax.fori_loop(0, blocks, backward, 0)


def layers(part, halo_ends, arrived, mine, other, head_bias, hs, slope_scale):
    micros, sides, count, _ = part.shape
    ends = micros * sides * count
    blocks = 2 * mine.shape[0] * hs // HID_BLOCK
    shape = jax.ShapeDtypeStruct(mine.shape, f32)
    return pl.pallas_call(
        lambda *refs: layers_kernel(*refs, hs=hs, slope_scale=slope_scale),
        out_shape=[shape, shape, jax.ShapeDtypeStruct((HALF + 8, LANES), f32)],
        scratch_shapes=[
            pltpu.VMEM((ends, 2 * LANES), bf16),
            pltpu.VMEM((2 * LANES, ends), bf16),
            pltpu.VMEM((blocks, 2 * HID_BLOCK, ends), bf16),
            pltpu.VMEM((LANES, ends), f32),
            pltpu.VMEM((4 * HALF, ends), bf16),
            pltpu.VMEM((ends, LANES), bf16),
        ],
        name="layers",
    )(part, halo_ends, arrived, mine, other, head_bias)


def stages(size):
    found = []
    stride = 1
    while stride < size:
        radix = min(4, size // stride)
        found.append((stride, radix))
        stride *= radix
    return found


def trade(x, offset):
    size = lax.axis_size("dom")
    return lax.ppermute(x, "dom", [(i, i ^ offset) for i in range(size)])


def swap(x):
    return lax.ppermute(x, "rep", [(0, 1), (1, 0)])


def spread(x):
    x = x[None]
    for stride, radix in reversed(stages(lax.axis_size("dom"))):
        x = jnp.concatenate([x] + [trade(x, stride * k) for k in range(1, radix)], axis=0)
    return x, swap(x)


def collect(mine, other):
    x = mine + swap(other)
    for stride, radix in stages(lax.axis_size("dom")):
        parts = x.reshape((radix, x.shape[0] // radix) + x.shape[1:])
        y = parts[0]
        for k in range(1, radix):
            y = y + trade(parts[k], stride * k)
        x = y
    return x[0]


def pack_shard(w_one, b_one, w_two):
    hs = b_one.shape[0]
    first = jnp.concatenate([w_one.T, b_one[:, None]], axis=1)
    first = jnp.pad(first, ((0, 0), (0, LANES - first.shape[1])))
    if hs % GROUP:
        head = jnp.pad(w_two, ((0, 0), (0, LANES - w_two.shape[1])))
    else:
        head = jnp.pad(w_two, ((0, 0), (0, HALF - w_two.shape[1])))
        head = jnp.concatenate([head[: hs // 2], head[hs // 2 :]], axis=1)
    return jnp.concatenate([first, head], axis=0)


def unpack_shard(g, hs, classes):
    head = g[hs:]
    if hs % GROUP == 0:
        head = jnp.concatenate([head[:, :HALF], head[:, HALF:]], axis=0)
    return g[:hs, :F].T, g[:hs, F], head[:, :classes]


def global_sum(x):
    count = lax.axis_size("dom") * lax.axis_size("rep")
    size = -(-x.shape[0] // LANES)
    x = jnp.pad(x, (0, size * LANES - x.shape[0])).reshape(1, size, LANES)
    x = jnp.broadcast_to(x, (count, size, LANES))
    return jnp.sum(lax.all_to_all(x, ("dom", "rep"), 0, 0, tiled=True), axis=0).reshape(-1)


def local(
    features,
    neighbors,
    nbr_mask,
    send_rows,
    halo_count,
    pos_edges,
    neg_edges,
    w_one,
    b_one,
    w_two,
    b_two,
    w_one_row,
    w_one_col,
    w_two_row,
    w_two_col,
    b_one_second,
    b_two_second,
):
    peers = lax.axis_size("dom")
    ranks = lax.axis_size("rep")
    micros, rows, _ = features.shape
    classes = w_two.shape[1]
    hs = b_one.shape[0]
    hidden_units = hs * peers * ranks
    slots = peers * HCAP
    total_edges = pos_edges.shape[1] * peers * micros * ranks
    degree = neighbors.shape[2]

    mine, other = spread(pack_shard(w_one, b_one, w_two))

    x = jnp.concatenate([features, jnp.ones((micros, rows, 1), f32)], axis=2)
    x = jnp.pad(x, ((0, 0), (0, 0), (0, LANES - F - 1)))
    valid = (jnp.arange(HCAP) < halo_count[..., None]).astype(f32)

    def exchange(values):
        sent = jnp.stack([values[m][send_rows[m]] for m in range(micros)], axis=1)
        sent = sent * jnp.moveaxis(valid, 0, 1)[..., None]
        return lax.all_to_all(sent, "dom", 0, 0, tiled=True)

    arrived_x = exchange(x)
    width = GROUP * degree
    sums, halo = local_sums(
        neighbors.reshape(micros, rows // GROUP, width),
        nbr_mask.reshape(micros, rows // GROUP, width),
        x,
        slots,
    )
    agg = finish(sums, halo, arrived_x)
    arrived_agg = exchange(agg)
    edges = jnp.concatenate([pos_edges, neg_edges], axis=1)
    ends = jnp.moveaxis(edges, 2, 1)[..., None]
    part = pick(ends, agg)
    head_bias = jnp.pad(b_two, (0, HALF - classes))[:, None]
    grad_mine, grad_other, stats = layers(
        part, ends[:, 1] - rows, arrived_agg, mine, other, head_bias, hs, 1.0 / (2.0 * total_edges)
    )
    g_one, gb_one, g_two = unpack_shard(collect(grad_mine, grad_other), hs, classes)

    decay = 1.0 - f32(STEP) ** (-0.8)
    square = g_one * g_one
    square_two = g_two * g_two
    row_part = jnp.sum(square + tiny_eps, axis=1)
    col_one = decay * w_one_col + (1.0 - decay) * jnp.sum(square + tiny_eps, axis=0)
    row_two = decay * w_two_row + (1.0 - decay) * jnp.sum(square_two + tiny_eps, axis=1)
    col_part = jnp.sum(square_two + tiny_eps, axis=0)
    second_one = decay * b_one_second + (1.0 - decay) * (gb_one * gb_one + tiny_eps)
    step_bias = gb_one * lax.rsqrt(second_one)
    scalars = jnp.stack(
        [
            jnp.sum(row_two),
            jnp.sum(w_one * w_one),
            jnp.sum(w_two * w_two),
            jnp.sum(b_one * b_one),
            jnp.sum(step_bias * step_bias),
            stats[HALF, 0],
        ]
    )
    pieces = [
        row_part,
        jnp.sum(square / col_one[None, :], axis=1),
        col_part,
        jnp.sum(square_two / row_two[:, None], axis=0),
        stats[:classes, 0],
        scalars,
    ]
    sums = global_sum(jnp.concatenate(pieces))
    found = []
    start = 0
    for piece in pieces:
        found.append(sums[start : start + piece.shape[0]])
        start += piece.shape[0]
    row_sum, row_scaled, col_sum, col_scaled, gb_two, scalars = found
    row_two_total, total_one, total_two, total_bias, rms_bias, loss_total = scalars
    loss = loss_total / (2.0 * total_edges)
    row_one = decay * w_one_row + (1.0 - decay) * row_sum
    col_two = decay * w_two_col + (1.0 - decay) * col_sum
    second_two = decay * b_two_second + (1.0 - decay) * (gb_two * gb_two + tiny_eps)
    row_one_total = jnp.sum(row_one)
    rms_one = jnp.sum(row_scaled / row_one) * row_one_total
    rms_two = jnp.sum(col_scaled / col_two) * row_two_total
    step_one = g_one * lax.rsqrt(jnp.outer(row_one, col_one) / row_one_total)
    step_two = g_two * lax.rsqrt(jnp.outer(row_two, col_two) / row_two_total)
    step_head = gb_two * lax.rsqrt(second_two)

    def clip(step, mean):
        return step / jnp.maximum(1.0, jnp.sqrt(mean) / clip_limit)

    step_one = clip(step_one, rms_one / (F * hidden_units))
    step_two = clip(step_two, rms_two / (hidden_units * classes))
    step_bias = clip(step_bias, rms_bias / hidden_units)
    step_head = clip(step_head, jnp.mean(step_head * step_head))

    def moved(old, mean, step):
        return old - step_rate * jnp.maximum(scale_eps, jnp.sqrt(mean)) * step

    return (
        loss,
        g_one,
        moved(w_one, total_one / (F * hidden_units), step_one),
        row_one,
        col_one,
        g_two,
        moved(w_two, total_two / (hidden_units * classes), step_two),
        row_two,
        col_two,
        gb_one,
        moved(b_one, total_bias / hidden_units, step_bias),
        second_one,
        gb_two,
        moved(b_two, jnp.mean(b_two * b_two), step_head),
        second_two,
    )


def solution(mesh):
    return jax.shard_map(
        local,
        mesh=mesh,
        in_specs=(
            P("rep", "dom", None),
            P("rep", "dom", None),
            P("rep", "dom", None),
            P("rep", "dom", None),
            P("rep", "dom"),
            P("rep", "dom", None),
            P("rep", "dom", None),
            P(None, ("dom", "rep")),
            P(("dom", "rep")),
            P(("dom", "rep"), None),
            P(),
            P(),
            P(("dom", "rep")),
            P(("dom", "rep")),
            P(),
            P(("dom", "rep")),
            P(),
        ),
        out_specs=(
            P(),
            P(None, ("dom", "rep")),
            P(None, ("dom", "rep")),
            P(),
            P(("dom", "rep")),
            P(("dom", "rep"), None),
            P(("dom", "rep"), None),
            P(("dom", "rep")),
            P(),
            P(("dom", "rep")),
            P(("dom", "rep")),
            P(("dom", "rep")),
            P(),
            P(),
            P(),
        ),
        check_vma=False,
    )
```

```python
import jax
import jax.numpy as jnp
from jax import lax
from jax.experimental import pallas as pl
from jax.experimental.pallas import tpu as pltpu
from jax.sharding import PartitionSpec as P

F = 100
HCAP = 8
STEP = 20
LANES = 128
HALF = 64
GROUP = 16
NODE_BLOCK = 256
HID_BLOCK = 256
COL_BLOCK = 512

tiny_eps = 1e-30
scale_eps = 0.001
clip_limit = 1.0
step_rate = 0.3
keep_rate = 1.0 - STEP**-0.8
new_rate = STEP**-0.8
f32 = jnp.float32
bf16 = jnp.bfloat16


def dot(a, b, dims=((1,), (0,))):
    return lax.dot_general(a, b, (dims, ((), ())), preferred_element_type=f32)


def split(x):
    hi = x.astype(bf16)
    lo = (x - hi.astype(f32)).astype(bf16)
    return hi, lo


def iota(shape, dim):
    return lax.broadcasted_iota(jnp.int32, shape, dim)


def one_hot(cond):
    return jnp.where(cond, 1.0, 0.0).astype(bf16)


def picked(table, index, base=0):
    which = one_hot(iota((table.shape[1], index.shape[1]), 0) + base == index)
    both = dot(table, which)
    return both[:LANES] + both[LANES:]


def sent_rows(table, index, out_ref, micro):
    rows = picked(table, index).T
    out_ref[:, micro] = rows.reshape(out_ref.shape[0], HCAP, LANES)


def front_kernel(x_ref, send_ref, table_ref, out_ref, full):
    full[...] = jnp.where(iota(full.shape, 0) == F, 1.0, 0.0)
    for m in range(send_ref.shape[0]):
        full[:F] = x_ref[:, m, :]
        hi, lo = split(full[...])
        table_ref[m, :LANES] = hi
        table_ref[m, LANES:] = lo
        sent_rows(table_ref[m], send_ref[m], out_ref, m)


def front(x, send):
    _, micros, rows = x.shape
    peers = send.shape[2] // HCAP
    return pl.pallas_call(
        front_kernel,
        out_shape=[
            jax.ShapeDtypeStruct((micros, 2 * LANES, rows), bf16),
            jax.ShapeDtypeStruct((peers, micros, HCAP, LANES), f32),
        ],
        scratch_shapes=[pltpu.VMEM((LANES, rows), f32)],
        name="front",
    )(x, send)


def local_sum_kernel(idx_ref, mask_ref, table_ref, sum_ref, halo_ref, counts):
    rows = table_ref.shape[2]
    high = counts.shape[1] // LANES
    degree, nodes = idx_ref.shape[1:]
    groups = nodes // GROUP
    v = jnp.where(mask_ref[0] > 0, idx_ref[0], counts.shape[1])
    lane_part = iota((degree, nodes), 1) // GROUP
    row = iota((degree, nodes), 0)
    turned = v
    for d in range(1, GROUP):
        moved = pltpu.roll(pltpu.roll(v, d, 0), nodes - GROUP * d, 1)
        turned = jnp.where(lane_part == ((row - d) & (GROUP - 1)), moved, turned)
    high_part = (turned >> 7).astype(f32)
    low_part = (turned & (LANES - 1)).astype(f32)
    width = degree * GROUP
    same = (iota((GROUP, width), 1) & (GROUP - 1)) == iota((GROUP, width), 0)
    same = jnp.where(same, 1.0, 0.0).astype(bf16)
    none = jnp.zeros((GROUP, width), bf16)
    low_rows = iota((LANES, width), 0).astype(f32).astype(bf16)
    one = jnp.ones((LANES, width), bf16)
    zero = jnp.zeros((LANES, width), bf16)
    for g in range(groups):
        hi = jnp.broadcast_to(high_part[g : g + 1], (GROUP, width)).astype(bf16)
        lo = jnp.broadcast_to(low_part[g : g + 1], (LANES, width)).astype(bf16)
        left = jnp.concatenate([jnp.where(hi == h, same, none) for h in range(high)], axis=0)
        right = jnp.where(low_rows == lo, one, zero)
        found = dot(left, right, ((1,), (1,))).astype(bf16)
        for h in range(high):
            counts[g * GROUP : (g + 1) * GROUP, h * LANES : (h + 1) * LANES] = found[
                h * GROUP : (h + 1) * GROUP
            ]
    both = dot(table_ref[0], counts[:, :rows], ((1,), (1,)))
    at = pl.multiple_of(pl.program_id(0) * nodes, nodes)
    own = table_ref[0, :, pl.ds(at, nodes)].astype(f32)
    both = both + own
    sum_ref[...] = both[:LANES] + both[LANES:]
    halo_ref[...] = counts[:, rows:]


def local_sums(idx, mask, table, micro, slots):
    _, degree, rows = idx.shape
    return pl.pallas_call(
        local_sum_kernel,
        grid=(rows // NODE_BLOCK,),
        in_specs=[
            pl.BlockSpec((1, degree, NODE_BLOCK), lambda b: (micro, 0, b)),
            pl.BlockSpec((1, degree, NODE_BLOCK), lambda b: (micro, 0, b)),
            pl.BlockSpec((1, 2 * LANES, rows), lambda b: (micro, 0, 0)),
        ],
        out_specs=[
            pl.BlockSpec((LANES, NODE_BLOCK), lambda b: (0, b)),
            pl.BlockSpec((NODE_BLOCK, slots), lambda b: (b, 0)),
        ],
        out_shape=[
            jax.ShapeDtypeStruct((LANES, rows), f32),
            jax.ShapeDtypeStruct((rows, slots), bf16),
        ],
        scratch_shapes=[pltpu.VMEM((NODE_BLOCK, rows + slots), bf16)],
        name="local_sums",
    )(idx, mask, table)


def finish_kernel(*refs):
    micros = (len(refs) - 4) // 2
    sums, halos = refs[:micros], refs[micros : 2 * micros]
    arrived_ref, send_ref, table_ref, out_ref = refs[2 * micros :]
    for m in range(micros):
        hi, lo = arrived_table(arrived_ref, m, 1.0)
        counts = halos[m][...]
        total = sums[m][...] + dot(hi, counts, ((1,), (1,))) + dot(lo, counts, ((1,), (1,)))
        agg = total / total[F : F + 1]
        agg = jnp.where(iota(agg.shape, 0) == F, 1.0, agg)
        hi, lo = split(agg)
        table_ref[m, :LANES] = hi
        table_ref[m, LANES:] = lo
        sent_rows(table_ref[m], send_ref[m], out_ref, m)


def arrived_table(ref, micro, degree=None):
    slots = ref.shape[0] * HCAP
    rows = ref[:, micro].reshape(slots, LANES)
    if degree is not None:
        rows = jnp.where(iota(rows.shape, 1) == F, degree, rows)
    return split(rows.T)


def finish(sums, halos, arrived, send):
    micros = len(sums)
    rows = sums[0].shape[1]
    return pl.pallas_call(
        finish_kernel,
        out_shape=[
            jax.ShapeDtypeStruct((micros, 2 * LANES, rows), bf16),
            jax.ShapeDtypeStruct(arrived.shape, f32),
        ],
        name="finish",
    )(*sums, *halos, arrived, send)


def edge_row(pos_ref, neg_ref, micro, side):
    pos = pos_ref[micro, side : side + 1, :]
    return jnp.concatenate([pos, neg_ref[micro, side : side + 1, :]], axis=1)


def pick_kernel(pos_ref, neg_ref, table_ref, out_ref):
    count = 2 * pos_ref.shape[2]
    for m in range(pos_ref.shape[0]):
        for s in range(2):
            at = (2 * m + s) * count
            out_ref[:, at : at + count] = picked(table_ref[m], edge_row(pos_ref, neg_ref, m, s))


def pick(pos, neg, table):
    ends = pos.shape[0] * 4 * pos.shape[2]
    return pl.pallas_call(
        pick_kernel, out_shape=jax.ShapeDtypeStruct((LANES, ends), f32), name="pick"
    )(pos, neg, table)


def first_block(ref, start, shards, hs):
    return ref[pl.ds(start, shards), 0:hs, :].reshape(shards * hs, LANES)


def head_block(ref, start, shards, hs):
    if hs % GROUP:
        return ref[pl.ds(start, shards), hs : 2 * hs, :].reshape(shards * hs, LANES)
    half = hs // 2
    packed = ref[pl.ds(start, shards), hs : hs + half, :].reshape(shards * half, LANES)
    low = iota(packed.shape, 1) < HALF
    left = jnp.where(low, packed, 0.0).reshape(shards, half, LANES)
    right = jnp.where(low, pltpu.roll(packed, HALF, 1), 0.0).reshape(shards, half, LANES)
    return jnp.concatenate([left, right], axis=1).reshape(shards * hs, LANES)


def head_terms(block):
    hi = block.astype(bf16)
    rest = block - hi.astype(f32)
    return hi, (hi.astype(f32) + pltpu.roll(rest, HALF, 1)).astype(bf16)


def layers_kernel(
    part_ref, pos_ref, neg_ref, arrived_ref, mine_ref, other_ref, head_bias_ref,
    grad_mine_ref, grad_other_ref, stats_ref,
    agg_row, agg_col, hidden, out_col, dz_col, dz_row,
    *, hs, nodes, slope_scale,
):
    micros, sides, count = pos_ref.shape[0], 2, 2 * pos_ref.shape[2]
    ends = micros * sides * count
    shards = HID_BLOCK // hs
    blocks = mine_ref.shape[0] // shards

    for m in range(micros):
        far = jnp.concatenate(arrived_table(arrived_ref, m), axis=0)
        far = picked(far, edge_row(pos_ref, neg_ref, m, 1), nodes)
        for s in range(sides):
            at = (m * sides + s) * count
            cols = part_ref[:, at : at + count]
            if s == 1:
                cols = cols + far
            hi, lo = split(cols)
            agg_col[:LANES, at : at + count] = hi
            agg_col[LANES:, at : at + count] = lo
            hi, lo = split(cols.T)
            agg_row[at : at + count, :LANES] = hi
            agg_row[at : at + count, LANES:] = lo

    out_col[...] = jnp.zeros(out_col.shape, f32)

    for side, ref in enumerate((mine_ref, other_ref)):

        def forward(c, carry, ref=ref, side=side):
            first = first_block(ref, c * shards, shards, hs)
            hi, lo = split(first)
            both = jnp.concatenate([hi, lo], axis=1)
            head_hi, head_both = head_terms(head_block(ref, c * shards, shards, hs))
            head = jnp.concatenate([head_both, head_hi], axis=0)
            slot = side * blocks + c
            for n in range(0, ends, COL_BLOCK):
                cols = slice(n, n + COL_BLOCK)
                upper = agg_col[:LANES, cols]
                pre = dot(both, jnp.concatenate([upper, upper], axis=0))
                pre = pre + dot(hi, agg_col[LANES:, cols])
                act_hi, act_lo = split(jnp.maximum(pre, 0.0))
                hidden[slot, :HID_BLOCK, cols] = act_hi
                hidden[slot, HID_BLOCK:, cols] = act_lo
                act = jnp.concatenate([act_hi, act_lo], axis=0)
                out_col[:, cols] += dot(head, act, ((0,), (0,)))
            return carry

        lax.fori_loop(0, blocks, forward, 0)

    bias = head_bias_ref[...].T[:HALF, :1]
    loss = jnp.zeros((1, 1), f32)
    head_grad = jnp.zeros((HALF, 1), f32)
    sign = jnp.where(iota((1, count), 1) < count // 2, -1.0, 1.0)
    for m in range(micros):
        at = m * sides * count
        mid = at + count
        end = mid + count
        z_u = out_col[:HALF, at:mid] + out_col[HALF:, at:mid] + bias
        z_v = out_col[:HALF, mid:end] + out_col[HALF:, mid:end] + bias
        score = jnp.sum(z_u * z_v, axis=0, keepdims=True) * sign
        tail = jnp.exp(-jnp.abs(score))
        plus = jnp.maximum(score, 0.0) + jnp.log1p(tail)
        loss = loss + jnp.sum(plus, axis=1, keepdims=True)
        slope = sign * jax.nn.sigmoid(score) * slope_scale
        for start, grad in ((at, slope * z_v), (mid, slope * z_u)):
            stop = start + count
            head_grad = head_grad + jnp.sum(grad, axis=1, keepdims=True)
            hi, lo = split(grad)
            dz_col[:HALF, start:stop] = hi
            dz_col[HALF : 2 * HALF, start:stop] = hi
            dz_col[2 * HALF : 3 * HALF, start:stop] = lo
            dz_col[3 * HALF :, start:stop] = jnp.zeros((HALF, count), bf16)
            both = jnp.concatenate([hi.astype(f32), lo.astype(f32)], axis=0)
            dz_row[start:stop] = both.T.astype(bf16)
    wide = jnp.broadcast_to(head_grad, (HALF, LANES))
    wide = jnp.concatenate([wide, jnp.broadcast_to(loss, (HALF, LANES))], axis=0)
    stats_ref[...] = wide.T[:8]

    for side, (ref, grad_ref) in enumerate(((mine_ref, grad_mine_ref), (other_ref, grad_other_ref))):

        def backward(c, carry, ref=ref, grad_ref=grad_ref, side=side):
            head_hi, head_both = head_terms(head_block(ref, c * shards, shards, hs))
            head = jnp.concatenate([head_both, head_hi], axis=1)
            slot = side * blocks + c
            head_sum = jnp.zeros((HID_BLOCK, LANES), f32)
            first_sum = jnp.zeros((HID_BLOCK, LANES), f32)
            for n in range(0, ends, COL_BLOCK):
                cols = slice(n, n + COL_BLOCK)
                act_hi = hidden[slot, :HID_BLOCK, cols]
                act_lo = hidden[slot, HID_BLOCK:, cols]
                grad = dot(head, dz_col[:, cols])
                grad = jnp.where(act_hi.astype(f32) > 0.0, grad, 0.0)
                hi, lo = split(grad)
                head_sum = head_sum + dot(act_hi, dz_row[cols]) + dot(act_lo, dz_row[cols])
                both = dot(hi, agg_row[cols])
                first_sum = first_sum + both[:, :LANES] + both[:, LANES:]
                first_sum = first_sum + dot(lo, agg_row[cols, :LANES])
            grad_ref[pl.ds(c * shards, shards), 0:hs, :] = first_sum.reshape(shards, hs, LANES)
            folded = (head_sum + pltpu.roll(head_sum, HALF, 1)).reshape(shards, hs, LANES)
            if hs % GROUP:
                grad_ref[pl.ds(c * shards, shards), hs : 2 * hs, :] = folded
            else:
                half = hs // 2
                low = iota((shards, half, LANES), 2) < HALF
                grad_ref[pl.ds(c * shards, shards), hs : hs + half, :] = jnp.where(
                    low, folded[:, :half], folded[:, half:]
                )
            return carry

        lax.fori_loop(0, blocks, backward, 0)


def layers(part, pos, neg, arrived, mine, other, head_bias, hs, nodes, slope_scale):
    ends = part.shape[1]
    blocks = 2 * mine.shape[0] * hs // HID_BLOCK
    shape = jax.ShapeDtypeStruct(mine.shape, f32)
    return pl.pallas_call(
        lambda *refs: layers_kernel(*refs, hs=hs, nodes=nodes, slope_scale=slope_scale),
        out_shape=[shape, shape, jax.ShapeDtypeStruct((8, LANES), f32)],
        scratch_shapes=[
            pltpu.VMEM((ends, 2 * LANES), bf16),
            pltpu.VMEM((2 * LANES, ends), bf16),
            pltpu.VMEM((blocks, 2 * HID_BLOCK, ends), bf16),
            pltpu.VMEM((LANES, ends), f32),
            pltpu.VMEM((4 * HALF, ends), bf16),
            pltpu.VMEM((ends, LANES), bf16),
        ],
        name="layers",
    )(part, pos, neg, arrived, mine, other, head_bias)


def stages(size):
    found = []
    stride = 1
    while stride < size:
        radix = min(4, size // stride)
        found.append((stride, radix))
        stride *= radix
    return found


def trade(x, offset):
    size = lax.axis_size("dom")
    return lax.ppermute(x, "dom", [(i, i ^ offset) for i in range(size)])


def swap(x):
    return lax.ppermute(x, "rep", [(0, 1), (1, 0)])


def spread_stage(x, stride, radix):
    return jnp.concatenate([x] + [trade(x, stride * k) for k in range(1, radix)], axis=0)


def collect(mine, other):
    x = mine + swap(other)
    for stride, radix in stages(lax.axis_size("dom")):
        parts = x.reshape((radix, x.shape[0] // radix) + x.shape[1:])
        y = parts[0]
        for k in range(1, radix):
            y = y + trade(parts[k], stride * k)
        x = y
    return x[0]


def pack_shard(w_one, b_one, w_two):
    hs = b_one.shape[0]
    first = jnp.concatenate([w_one.T, b_one[:, None]], axis=1)
    first = jnp.pad(first, ((0, 0), (0, LANES - first.shape[1])))
    if hs % GROUP:
        head = jnp.pad(w_two, ((0, 0), (0, LANES - w_two.shape[1])))
    else:
        head = jnp.pad(w_two, ((0, 0), (0, HALF - w_two.shape[1])))
        head = jnp.concatenate([head[: hs // 2], head[hs // 2 :]], axis=1)
    return jnp.concatenate([first, head], axis=0)


def unpack_head(g, hs):
    head = g[hs:]
    if hs % GROUP:
        return head
    low = iota((hs // 2, LANES), 1) < HALF
    right = jnp.where(low, pltpu.roll(head, HALF, 1), 0.0)
    return jnp.concatenate([jnp.where(low, head, 0.0), right], axis=0)


def to_column(row, hs):
    wide = jnp.broadcast_to(row, (8, row.shape[1]))
    if row.shape[1] < LANES:
        wide = jnp.concatenate([wide, jnp.zeros((8, LANES - row.shape[1]), f32)], axis=1)
    return wide.T[:hs, :1]


def total(x):
    return jnp.sum(jnp.sum(x, axis=1, keepdims=True), axis=0, keepdims=True)


def stats_kernel(
    g_ref, stats_ref, w_one_ref, b_one_ref, w_two_ref, col_ref, row_ref, second_ref,
    g_one_ref, g_two_ref, g_bias_ref, col_new_ref, row_new_ref, second_new_ref,
    step_one_ref, step_two_ref, sums_ref,
):
    hs = b_one_ref.shape[1]
    classes = w_two_ref.shape[0]
    g = g_ref[...]
    one = g[:hs]
    one_t = one.T
    two = unpack_head(g, hs)
    two_t = two.T
    feature = iota((hs, LANES), 1) < F
    label = iota((hs, LANES), 1) < classes
    g_one_ref[...] = one[:, :F]
    g_two_ref[...] = two_t[:classes]
    g_bias = one_t[F : F + 1]
    g_bias_ref[...] = g_bias
    square = jnp.where(feature, one * one + tiny_eps, 0.0)
    square_t = jnp.where(iota((LANES, hs), 0) < F, one_t * one_t + tiny_eps, 0.0)
    two_square = jnp.where(label, two * two + tiny_eps, 0.0)
    two_square_t = jnp.where(iota((LANES, hs), 0) < classes, two_t * two_t + tiny_eps, 0.0)
    col_new = keep_rate * col_ref[...] + new_rate * jnp.sum(square_t, axis=0, keepdims=True)
    row_new = keep_rate * row_ref[...] + new_rate * jnp.sum(two_square_t, axis=0, keepdims=True)
    second_new = keep_rate * second_ref[...] + new_rate * (g_bias * g_bias + tiny_eps)
    col_new_ref[...] = col_new
    row_new_ref[...] = row_new
    second_new_ref[...] = second_new
    step_one = one * lax.rsqrt(to_column(col_new, hs))
    step_one = jnp.where(feature, step_one, 0.0)
    step_one_ref[...] = step_one
    step_two_ref[...] = two_t * lax.rsqrt(row_new)
    step_two = jnp.where(label, two * lax.rsqrt(to_column(row_new, hs)), 0.0)
    step_bias = g_bias * lax.rsqrt(second_new)
    w_one = w_one_ref[...]
    w_two = w_two_ref[...]
    b_one = b_one_ref[...]
    lane = iota((1, LANES), 1)
    scalars = [
        total(row_new),
        total(w_one * w_one),
        total(w_two * w_two),
        total(b_one * b_one),
        total(step_bias * step_bias),
        stats_ref[0:1, HALF : HALF + 1],
    ]
    first = jnp.sum(square, axis=0, keepdims=True)
    for i, value in enumerate(scalars):
        first = jnp.where(lane == F + 1 + i, value, first)
    head = jnp.sum(step_two * step_two, axis=0, keepdims=True)
    sums = jnp.concatenate(
        [
            first,
            jnp.sum(step_one * step_one, axis=0, keepdims=True),
            jnp.sum(two_square, axis=0, keepdims=True) + pltpu.roll(jnp.broadcast_to(head, (8, LANES)), HALF, 1)[:1],
            jnp.where(lane < HALF, stats_ref[0:1], 0.0),
        ],
        axis=0,
    )
    sums_ref[...] = jnp.broadcast_to(sums[None], sums_ref.shape)


def update_kernel(
    sums_ref, step_one_ref, step_two_ref, g_bias_ref, second_new_ref,
    w_one_ref, b_one_ref, w_two_ref, b_two_ref, row_ref, col_ref, second_ref,
    loss_ref, w_one_new_ref, row_new_ref, w_two_new_ref, col_new_ref, b_one_new_ref,
    g_head_ref, b_two_new_ref, second_new_head_ref,
    *, hidden_units, slope_scale,
):
    hs = b_one_ref.shape[1]
    classes = w_two_ref.shape[0]
    sums = jnp.sum(sums_ref[...], axis=0)
    row_total, one_total, two_total, bias_total, bias_rms, loss = [
        sums[0:1, F + 1 + i : F + 2 + i] for i in range(6)
    ]
    loss_ref[...] = loss * slope_scale
    row_new = keep_rate * row_ref[...] + new_rate * sums[0:1, :F]
    row_new_ref[...] = row_new
    col_new = keep_rate * col_ref[...] + new_rate * sums[2:3, :classes]
    col_new_ref[...] = col_new
    g_head = sums[3:4, :classes]
    g_head_ref[...] = g_head
    second = keep_rate * second_ref[...] + new_rate * (g_head * g_head + tiny_eps)
    second_new_head_ref[...] = second

    def clip(mean):
        return 1.0 / jnp.maximum(1.0, jnp.sqrt(mean) / clip_limit)

    def rate(mean):
        return step_rate * jnp.maximum(scale_eps, jnp.sqrt(mean))

    row_sum = jnp.sum(row_new, axis=1, keepdims=True)
    one_rms = jnp.sum(sums[1:2, :F] / row_new, axis=1, keepdims=True) * row_sum
    head_sums = pltpu.roll(jnp.broadcast_to(sums[2:3], (8, LANES)), HALF, 1)[:1, :classes]
    two_rms = jnp.sum(head_sums / col_new, axis=1, keepdims=True) * row_total
    one_rate = clip(one_rms / (F * hidden_units)) * rate(one_total / (F * hidden_units))
    step_one = step_one_ref[:, :F] * lax.rsqrt(row_new / row_sum)
    w_one_new_ref[...] = w_one_ref[...] - one_rate * step_one
    size = hidden_units * classes
    two_rate = clip(two_rms / size) * rate(two_total / size)
    scale = to_column(lax.rsqrt(col_new / row_total), classes)
    w_two_new_ref[...] = w_two_ref[...] - two_rate * (step_two_ref[:classes] * scale)
    bias_rate = clip(bias_rms / hidden_units) * rate(bias_total / hidden_units)
    b_one_new_ref[...] = b_one_ref[...] - bias_rate * (g_bias_ref[...] * lax.rsqrt(second_new_ref[...]))
    step_head = g_head * lax.rsqrt(second)
    b_two = b_two_ref[...]
    head_rate = clip(jnp.sum(step_head * step_head, axis=1, keepdims=True) / classes)
    head_rate = head_rate * rate(jnp.sum(b_two * b_two, axis=1, keepdims=True) / classes)
    b_two_new_ref[...] = b_two - head_rate * step_head


def local(
    features,
    neighbors,
    nbr_mask,
    send_rows,
    halo_count,
    pos_edges,
    neg_edges,
    w_one,
    b_one,
    w_two,
    b_two,
    w_one_row,
    w_one_col,
    w_two_row,
    w_two_col,
    b_one_second,
    b_two_second,
):
    peers = lax.axis_size("dom")
    ranks = lax.axis_size("rep")
    micros, rows, _ = features.shape
    classes = w_two.shape[1]
    hs = b_one.shape[0]
    slots = peers * HCAP
    total_edges = pos_edges.shape[1] * peers * micros * ranks

    x = jnp.transpose(features, (2, 0, 1))
    idx = jnp.transpose(neighbors, (0, 2, 1))
    mask = jnp.transpose(nbr_mask, (0, 2, 1))
    pos = jnp.transpose(pos_edges, (0, 2, 1))
    neg = jnp.transpose(neg_edges, (0, 2, 1))
    send = jnp.where(jnp.arange(HCAP) < halo_count[..., None], send_rows, -1)
    send = send.reshape(micros, 1, slots)
    slope_scale = 1.0 / (2.0 * total_edges)

    def exchange(sent):
        return lax.all_to_all(sent, "dom", 0, 0, tiled=True)

    table, sent = front(x, send)
    arrived_x = exchange(sent)
    weights = pack_shard(w_one, b_one, w_two)[None]
    sums, halos = [], []
    turns = list(reversed(stages(peers)))
    for m in range(micros):
        if m < len(turns):
            weights = spread_stage(weights, *turns[m])
        total_rows, halo = local_sums(idx, mask, table, m, slots)
        if m + 1 < len(turns):
            total_rows, weights, table = lax.optimization_barrier((total_rows, weights, table))
        sums.append(total_rows)
        halos.append(halo)
    for turn in turns[micros:]:
        weights = spread_stage(weights, *turn)
    other = swap(weights)
    table, sent = finish(sums, halos, arrived_x, send)
    arrived_agg = exchange(sent)
    part = pick(pos, neg, table)
    head_bias = jnp.broadcast_to(jnp.pad(b_two, (0, LANES - classes)), (8, LANES))
    grad_mine, grad_other, stats = layers(
        part, pos, neg, arrived_agg, weights, other, head_bias, hs, rows, slope_scale
    )
    g = collect(grad_mine, grad_other)

    w_one_t = w_one.T
    w_two_t = w_two.T
    b_one_row = b_one[None]

    def out(*shape):
        return jax.ShapeDtypeStruct(shape, f32)

    vec = out(1, hs)
    count = peers * ranks
    g_one, g_two, g_bias, col_one, row_two, second_one, step_one, step_two, parts = pl.pallas_call(
        stats_kernel,
        out_shape=[
            out(hs, F), out(classes, hs), vec, vec, vec, vec,
            out(hs, LANES), out(LANES, hs), out(count, 4, LANES),
        ],
        name="stats",
    )(g, stats, w_one_t, b_one_row, w_two_t, w_one_col[None], w_two_row[None], b_one_second[None])
    parts = lax.all_to_all(parts, ("dom", "rep"), 0, 0, tiled=True)
    head = out(1, classes)
    loss, w_one_new, row_one, w_two_new, col_two, b_one_new, g_head, b_two_new, second_two = pl.pallas_call(
        lambda *refs: update_kernel(
            *refs, hidden_units=hs * count, slope_scale=slope_scale
        ),
        out_shape=[
            out(1, 1), out(hs, F), out(1, F), out(classes, hs), head, vec, head, head, head,
        ],
        name="update",
    )(
        parts, step_one, step_two, g_bias, second_one,
        w_one_t, b_one_row, w_two_t, b_two[None], w_one_row[None], w_two_col[None], b_two_second[None],
    )
    return (
        loss[0, 0],
        g_one.T,
        w_one_new.T,
        row_one[0],
        col_one[0],
        g_two.T,
        w_two_new.T,
        row_two[0],
        col_two[0],
        g_bias[0],
        b_one_new[0],
        second_one[0],
        g_head[0],
        b_two_new[0],
        second_two[0],
    )


def solution(mesh):
    return jax.shard_map(
        local,
        mesh=mesh,
        in_specs=(
            P("rep", "dom", None),
            P("rep", "dom", None),
            P("rep", "dom", None),
            P("rep", "dom", None),
            P("rep", "dom"),
            P("rep", "dom", None),
            P("rep", "dom", None),
            P(None, ("dom", "rep")),
            P(("dom", "rep")),
            P(("dom", "rep"), None),
            P(),
            P(),
            P(("dom", "rep")),
            P(("dom", "rep")),
            P(),
            P(("dom", "rep")),
            P(),
        ),
        out_specs=(
            P(),
            P(None, ("dom", "rep")),
            P(None, ("dom", "rep")),
            P(),
            P(("dom", "rep")),
            P(("dom", "rep"), None),
            P(("dom", "rep"), None),
            P(("dom", "rep")),
            P(),
            P(("dom", "rep")),
            P(("dom", "rep")),
            P(("dom", "rep")),
            P(),
            P(),
            P(),
        ),
        check_vma=False,
    )
```

```python
import jax
import jax.numpy as jnp
from jax import lax
from jax.experimental import pallas as pl
from jax.experimental.pallas import tpu as pltpu
from jax.sharding import PartitionSpec as P

F = 100
HCAP = 8
STEP = 20
LANES = 128
HALF = 64
GROUP = 16
HID_BLOCK = 256
COL_BLOCK = 512

tiny_eps = 1e-30
scale_eps = 0.001
clip_limit = 1.0
step_rate = 0.3
keep_rate = 1.0 - STEP**-0.8
new_rate = STEP**-0.8
f32 = jnp.float32
bf16 = jnp.bfloat16


def dot(a, b, dims=((1,), (0,))):
    return lax.dot_general(a, b, (dims, ((), ())), preferred_element_type=f32)


def split(x):
    hi = x.astype(bf16)
    lo = (x - hi.astype(f32)).astype(bf16)
    return hi, lo


def iota(shape, dim):
    return lax.broadcasted_iota(jnp.int32, shape, dim)


def one_hot(cond):
    return jnp.where(cond, 1.0, 0.0).astype(bf16)


def picked(table, index, base=0):
    which = one_hot(iota((table.shape[1], index.shape[1]), 0) + base == index)
    both = dot(table, which)
    return both[:LANES] + both[LANES:]


def sent_rows(table, index, out_ref, micro):
    rows = picked(table, index).T
    out_ref[:, micro] = rows.reshape(out_ref.shape[0], HCAP, LANES)


def front_kernel(x_ref, send_ref, table_ref, out_ref, full):
    full[...] = jnp.where(iota(full.shape, 0) == F, 1.0, 0.0)
    for m in range(send_ref.shape[0]):
        full[:F] = x_ref[:, m, :]
        hi, lo = split(full[...])
        table_ref[m, :LANES] = hi
        table_ref[m, LANES:] = lo
        sent_rows(table_ref[m], send_ref[m], out_ref, m)


def front(x, send):
    _, micros, rows = x.shape
    peers = send.shape[2] // HCAP
    return pl.pallas_call(
        front_kernel,
        out_shape=[
            jax.ShapeDtypeStruct((micros, 2 * LANES, rows), bf16),
            jax.ShapeDtypeStruct((peers, micros, HCAP, LANES), f32),
        ],
        scratch_shapes=[pltpu.VMEM((LANES, rows), f32)],
        name="front",
    )(x, send)


def arrived_table(ref, micro, degree=None):
    slots = ref.shape[0] * HCAP
    rows = ref[:, micro].reshape(slots, LANES)
    if degree is not None:
        rows = jnp.where(iota(rows.shape, 1) == F, degree, rows)
    return jnp.concatenate(split(rows.T), axis=0)


def edge_row(pos_ref, neg_ref, micro, side):
    pos = pos_ref[micro, side : side + 1, :]
    return jnp.concatenate([pos, neg_ref[micro, side : side + 1, :]], axis=1)


def select_kernel(
    idx_ref, mask_ref, table_ref, send_ref, pos_ref, neg_ref,
    sent_slot_ref, sent_own_ref, slot_ref, own_ref, wide,
):
    degree = idx_ref.shape[1]
    for m in range(idx_ref.shape[0]):
        slot = jnp.where(mask_ref[m] > 0, idx_ref[m] + 1, 0)
        wide[:degree] = (slot >> 8).astype(f32).astype(bf16)
        wide[degree : 2 * degree] = (slot & 255).astype(f32).astype(bf16)
        wide[2 * degree :] = table_ref[m]
        count = 2 * pos_ref.shape[2]
        ends = [(edge_row(pos_ref, neg_ref, m, k), slot_ref, own_ref, k * count) for k in range(2)]
        for index, slots, owns, at in [(send_ref[m], sent_slot_ref, sent_own_ref, 0)] + ends:
            stop = at + index.shape[1]
            which = one_hot(iota((wide.shape[1], index.shape[1]), 0) == index)
            found = dot(wide[...], which)
            high = found[:degree].astype(jnp.int32)
            slots[m, :, at:stop] = high * 256 + found[degree : 2 * degree].astype(jnp.int32)
            own = found[2 * degree :]
            owns[m, :, at:stop] = own[:LANES] + own[LANES:]


def select(idx, mask, table, send, pos, neg):
    micros, degree, rows = idx.shape
    shapes = []
    for count in (send.shape[2], 4 * pos.shape[2]):
        shapes.append(jax.ShapeDtypeStruct((micros, degree, count), jnp.int32))
        shapes.append(jax.ShapeDtypeStruct((micros, LANES, count), f32))
    return pl.pallas_call(
        select_kernel,
        out_shape=shapes,
        scratch_shapes=[pltpu.VMEM((2 * degree + 2 * LANES, rows), bf16)],
        name="select",
    )(idx, mask, table, send, pos, neg)


def count_slots(slots, counts):
    degree, nodes = slots.shape
    width = degree * GROUP
    span = 2 * LANES
    high = -(-counts.shape[1] // span)
    slots = slots - 1
    lane_part = iota((degree, width), 1) // GROUP
    row = iota((degree, width), 0)
    parts = []
    for at in range(0, nodes, width):
        size = min(width, nodes - at)
        piece = slots[:, at : at + size]
        if size < width:
            piece = jnp.concatenate([piece, jnp.full((degree, width - size), -1, jnp.int32)], axis=1)
        turned = piece
        for d in range(1, GROUP):
            moved = pltpu.roll(pltpu.roll(piece, d, 0), width - GROUP * d, 1)
            turned = jnp.where(lane_part == ((row - d) & (GROUP - 1)), moved, turned)
        parts.append(turned)
    turned = jnp.concatenate(parts, axis=0)
    high_part = (turned >> 8).astype(f32)
    low_part = (turned & (span - 1)).astype(f32)
    same = (iota((GROUP, width), 1) & (GROUP - 1)) == iota((GROUP, width), 0)
    same = one_hot(same)
    none = jnp.zeros((GROUP, width), bf16)
    low_rows = iota((span, width), 0).astype(f32).astype(bf16)
    one = jnp.ones((span, width), bf16)
    zero = jnp.zeros((span, width), bf16)
    for g in range(nodes // GROUP):
        hi = jnp.broadcast_to(high_part[g : g + 1], (GROUP, width)).astype(bf16)
        lo = jnp.broadcast_to(low_part[g : g + 1], (span, width)).astype(bf16)
        left = jnp.concatenate([jnp.where(hi == h, same, none) for h in range(high)], axis=0)
        right = jnp.where(low_rows == lo, one, zero)
        found = dot(left, right, ((1,), (1,))).astype(bf16)
        for h in range(high):
            at = h * span
            size = min(span, counts.shape[1] - at)
            counts[g * GROUP : (g + 1) * GROUP, at : at + size] = found[
                h * GROUP : (h + 1) * GROUP, :size
            ]


def mean_columns(slots, own, table, arrived, counts):
    count_slots(slots, counts)
    rows = table.shape[1]
    both = dot(table, counts[:, :rows], ((1,), (1,)))
    both = both + dot(arrived, counts[:, rows:], ((1,), (1,)))
    total = both[:LANES] + both[LANES:] + own
    degree = total[F : F + 1]
    mean = jnp.where(degree > 0.5, total / jnp.maximum(degree, 1.0), 0.0)
    return jnp.where(iota(mean.shape, 0) == F, jnp.minimum(degree, 1.0), mean)


def mean_sent_kernel(slot_ref, own_ref, table_ref, arrived_ref, out_ref, counts):
    for m in range(slot_ref.shape[0]):
        arrived = arrived_table(arrived_ref, m, 1.0)
        mean = mean_columns(slot_ref[m], own_ref[m], table_ref[m], arrived, counts)
        out_ref[:, m] = mean.T.reshape(out_ref.shape[0], HCAP, LANES)


def mean_sent(slot, own, table, arrived):
    micros, degree, _ = slot.shape
    sent = arrived.shape[0] * HCAP
    rows = table.shape[2]
    return pl.pallas_call(
        mean_sent_kernel,
        grid=(1,),
        in_specs=[
            pl.BlockSpec((micros, degree, sent), lambda i: (0, 0, 0)),
            pl.BlockSpec((micros, LANES, sent), lambda i: (0, 0, 0)),
            pl.BlockSpec(table.shape, lambda i: (0, 0, 0)),
            pl.BlockSpec(arrived.shape, lambda i: (0, 0, 0, 0)),
        ],
        out_specs=pl.BlockSpec(arrived.shape, lambda i: (0, 0, 0, 0)),
        out_shape=jax.ShapeDtypeStruct(arrived.shape, f32),
        scratch_shapes=[pltpu.VMEM((sent, rows + sent), bf16)],
        name="mean_sent",
    )(slot, own, table, arrived)


def mean_ends_kernel(slot_ref, own_ref, table_ref, arrived_ref, out_ref, counts):
    arrived = arrived_table(arrived_ref, 0, 1.0)
    out_ref[...] = mean_columns(slot_ref[0], own_ref[0], table_ref[0], arrived, counts)


def mean_ends(slot, own, table, arrived, micro, block):
    degree = slot.shape[1]
    peers = arrived.shape[0]
    sent = peers * HCAP
    rows = table.shape[2]
    count = slot.shape[2]
    return pl.pallas_call(
        mean_ends_kernel,
        grid=(count // block,),
        in_specs=[
            pl.BlockSpec((1, degree, block), lambda b: (micro, 0, b)),
            pl.BlockSpec((1, LANES, block), lambda b: (micro, 0, b)),
            pl.BlockSpec((1, 2 * LANES, rows), lambda b: (micro, 0, 0)),
            pl.BlockSpec((peers, 1, HCAP, LANES), lambda b: (0, micro, 0, 0)),
        ],
        out_specs=pl.BlockSpec((LANES, block), lambda b: (0, b)),
        out_shape=jax.ShapeDtypeStruct((LANES, count), f32),
        scratch_shapes=[pltpu.VMEM((block, rows + sent), bf16)],
        name="mean_ends",
    )(slot, own, table, arrived)


def first_block(ref, start, shards, hs):
    return ref[pl.ds(start, shards), 0:hs, :].reshape(shards * hs, LANES)


def head_block(ref, start, shards, hs):
    if hs % GROUP:
        return ref[pl.ds(start, shards), hs : 2 * hs, :].reshape(shards * hs, LANES)
    half = hs // 2
    packed = ref[pl.ds(start, shards), hs : hs + half, :].reshape(shards * half, LANES)
    low = iota(packed.shape, 1) < HALF
    left = jnp.where(low, packed, 0.0).reshape(shards, half, LANES)
    right = jnp.where(low, pltpu.roll(packed, HALF, 1), 0.0).reshape(shards, half, LANES)
    return jnp.concatenate([left, right], axis=1).reshape(shards * hs, LANES)


def head_terms(block):
    hi = block.astype(bf16)
    rest = block - hi.astype(f32)
    return hi, (hi.astype(f32) + pltpu.roll(rest, HALF, 1)).astype(bf16)


def layers_kernel(
    *refs, hs, nodes, slope_scale,
):
    agg_row, agg_col, hidden, out_col, dz_col, dz_row = refs[-6:]
    grad_mine_ref, grad_other_ref, stats_ref = refs[-9:-6]
    pos_ref, neg_ref, arrived_ref, mine_ref, other_ref, head_bias_ref = refs[-15:-9]
    parts = refs[:-15]
    micros, sides, count = pos_ref.shape[0], 2, 2 * pos_ref.shape[2]
    ends = micros * sides * count
    shards = HID_BLOCK // hs
    blocks = mine_ref.shape[0] // shards

    for m in range(micros):
        far = picked(arrived_table(arrived_ref, m), edge_row(pos_ref, neg_ref, m, 1), nodes)
        for s in range(sides):
            at = (m * sides + s) * count
            cols = parts[m][:, s * count : (s + 1) * count]
            if s == 1:
                cols = cols + far
            hi, lo = split(cols)
            agg_col[:LANES, at : at + count] = hi
            agg_col[LANES:, at : at + count] = lo
            hi, lo = split(cols.T)
            agg_row[at : at + count, :LANES] = hi
            agg_row[at : at + count, LANES:] = lo

    out_col[...] = jnp.zeros(out_col.shape, f32)

    for side, ref in enumerate((mine_ref, other_ref)):

        def forward(c, carry, ref=ref, side=side):
            first = first_block(ref, c * shards, shards, hs)
            hi, lo = split(first)
            both = jnp.concatenate([hi, lo], axis=1)
            head_hi, head_both = head_terms(head_block(ref, c * shards, shards, hs))
            head = jnp.concatenate([head_both, head_hi], axis=0)
            slot = side * blocks + c
            for n in range(0, ends, COL_BLOCK):
                cols = slice(n, n + COL_BLOCK)
                upper = agg_col[:LANES, cols]
                pre = dot(both, jnp.concatenate([upper, upper], axis=0))
                pre = pre + dot(hi, agg_col[LANES:, cols])
                act_hi, act_lo = split(jnp.maximum(pre, 0.0))
                hidden[slot, :HID_BLOCK, cols] = act_hi
                hidden[slot, HID_BLOCK:, cols] = act_lo
                act = jnp.concatenate([act_hi, act_lo], axis=0)
                out_col[:, cols] += dot(head, act, ((0,), (0,)))
            return carry

        lax.fori_loop(0, blocks, forward, 0)

    bias = head_bias_ref[...].T[:HALF, :1]
    loss = jnp.zeros((1, 1), f32)
    head_grad = jnp.zeros((HALF, 1), f32)
    sign = jnp.where(iota((1, count), 1) < count // 2, -1.0, 1.0)
    for m in range(micros):
        at = m * sides * count
        mid = at + count
        end = mid + count
        z_u = out_col[:HALF, at:mid] + out_col[HALF:, at:mid] + bias
        z_v = out_col[:HALF, mid:end] + out_col[HALF:, mid:end] + bias
        score = jnp.sum(z_u * z_v, axis=0, keepdims=True) * sign
        tail = jnp.exp(-jnp.abs(score))
        plus = jnp.maximum(score, 0.0) + jnp.log1p(tail)
        loss = loss + jnp.sum(plus, axis=1, keepdims=True)
        slope = sign * jax.nn.sigmoid(score) * slope_scale
        for start, grad in ((at, slope * z_v), (mid, slope * z_u)):
            stop = start + count
            head_grad = head_grad + jnp.sum(grad, axis=1, keepdims=True)
            hi, lo = split(grad)
            dz_col[:HALF, start:stop] = hi
            dz_col[HALF : 2 * HALF, start:stop] = hi
            dz_col[2 * HALF : 3 * HALF, start:stop] = lo
            dz_col[3 * HALF :, start:stop] = jnp.zeros((HALF, count), bf16)
            both = jnp.concatenate([hi.astype(f32), lo.astype(f32)], axis=0)
            dz_row[start:stop] = both.T.astype(bf16)
    wide = jnp.broadcast_to(head_grad, (HALF, LANES))
    wide = jnp.concatenate([wide, jnp.broadcast_to(loss, (HALF, LANES))], axis=0)
    stats_ref[...] = wide.T[:8]

    for side, (ref, grad_ref) in enumerate(((mine_ref, grad_mine_ref), (other_ref, grad_other_ref))):

        def backward(c, carry, ref=ref, grad_ref=grad_ref, side=side):
            head_hi, head_both = head_terms(head_block(ref, c * shards, shards, hs))
            head = jnp.concatenate([head_both, head_hi], axis=1)
            slot = side * blocks + c
            head_sum = jnp.zeros((HID_BLOCK, LANES), f32)
            first_sum = jnp.zeros((HID_BLOCK, LANES), f32)
            for n in range(0, ends, COL_BLOCK):
                cols = slice(n, n + COL_BLOCK)
                act_hi = hidden[slot, :HID_BLOCK, cols]
                act_lo = hidden[slot, HID_BLOCK:, cols]
                grad = dot(head, dz_col[:, cols])
                grad = jnp.where(act_hi.astype(f32) > 0.0, grad, 0.0)
                hi, lo = split(grad)
                head_sum = head_sum + dot(act_hi, dz_row[cols]) + dot(act_lo, dz_row[cols])
                both = dot(hi, agg_row[cols])
                first_sum = first_sum + both[:, :LANES] + both[:, LANES:]
                first_sum = first_sum + dot(lo, agg_row[cols, :LANES])
            grad_ref[pl.ds(c * shards, shards), 0:hs, :] = first_sum.reshape(shards, hs, LANES)
            folded = (head_sum + pltpu.roll(head_sum, HALF, 1)).reshape(shards, hs, LANES)
            if hs % GROUP:
                grad_ref[pl.ds(c * shards, shards), hs : 2 * hs, :] = folded
            else:
                half = hs // 2
                low = iota((shards, half, LANES), 2) < HALF
                grad_ref[pl.ds(c * shards, shards), hs : hs + half, :] = jnp.where(
                    low, folded[:, :half], folded[:, half:]
                )
            return carry

        lax.fori_loop(0, blocks, backward, 0)


def layers(parts, pos, neg, arrived, mine, other, head_bias, hs, nodes, slope_scale):
    ends = len(parts) * parts[0].shape[1]
    blocks = 2 * mine.shape[0] * hs // HID_BLOCK
    shape = jax.ShapeDtypeStruct(mine.shape, f32)
    return pl.pallas_call(
        lambda *refs: layers_kernel(*refs, hs=hs, nodes=nodes, slope_scale=slope_scale),
        out_shape=[shape, shape, jax.ShapeDtypeStruct((8, LANES), f32)],
        scratch_shapes=[
            pltpu.VMEM((ends, 2 * LANES), bf16),
            pltpu.VMEM((2 * LANES, ends), bf16),
            pltpu.VMEM((blocks, 2 * HID_BLOCK, ends), bf16),
            pltpu.VMEM((LANES, ends), f32),
            pltpu.VMEM((4 * HALF, ends), bf16),
            pltpu.VMEM((ends, LANES), bf16),
        ],
        name="layers",
    )(*parts, pos, neg, arrived, mine, other, head_bias)


def stages(size):
    found = []
    stride = 1
    while stride < size:
        radix = min(4, size // stride)
        found.append((stride, radix))
        stride *= radix
    return found


def trade(x, offset):
    size = lax.axis_size("dom")
    return lax.ppermute(x, "dom", [(i, i ^ offset) for i in range(size)])


def swap(x):
    return lax.ppermute(x, "rep", [(0, 1), (1, 0)])


def spread_stage(x, stride, radix):
    return jnp.concatenate([x] + [trade(x, stride * k) for k in range(1, radix)], axis=0)


def collect(mine, other):
    x = mine + swap(other)
    for stride, radix in stages(lax.axis_size("dom")):
        parts = x.reshape((radix, x.shape[0] // radix) + x.shape[1:])
        y = parts[0]
        for k in range(1, radix):
            y = y + trade(parts[k], stride * k)
        x = y
    return x[0]


def pack_shard(w_one, b_one, w_two):
    hs = b_one.shape[0]
    first = jnp.concatenate([w_one.T, b_one[:, None]], axis=1)
    first = jnp.pad(first, ((0, 0), (0, LANES - first.shape[1])))
    if hs % GROUP:
        head = jnp.pad(w_two, ((0, 0), (0, LANES - w_two.shape[1])))
    else:
        head = jnp.pad(w_two, ((0, 0), (0, HALF - w_two.shape[1])))
        head = jnp.concatenate([head[: hs // 2], head[hs // 2 :]], axis=1)
    return jnp.concatenate([first, head], axis=0)


def unpack_head(g, hs):
    head = g[hs:]
    if hs % GROUP:
        return head
    low = iota((hs // 2, LANES), 1) < HALF
    right = jnp.where(low, pltpu.roll(head, HALF, 1), 0.0)
    return jnp.concatenate([jnp.where(low, head, 0.0), right], axis=0)


def to_column(row, hs):
    wide = jnp.broadcast_to(row, (8, row.shape[1]))
    if row.shape[1] < LANES:
        wide = jnp.concatenate([wide, jnp.zeros((8, LANES - row.shape[1]), f32)], axis=1)
    return wide.T[:hs, :1]


def total(x):
    return jnp.sum(jnp.sum(x, axis=1, keepdims=True), axis=0, keepdims=True)


def stats_kernel(
    g_ref, stats_ref, w_one_ref, b_one_ref, w_two_ref, col_ref, row_ref, second_ref,
    g_one_ref, g_two_ref, g_bias_ref, col_new_ref, row_new_ref, second_new_ref,
    step_one_ref, step_two_ref, sums_ref,
):
    hs = b_one_ref.shape[1]
    classes = w_two_ref.shape[0]
    g = g_ref[...]
    one = g[:hs]
    one_t = one.T
    two = unpack_head(g, hs)
    two_t = two.T
    feature = iota((hs, LANES), 1) < F
    label = iota((hs, LANES), 1) < classes
    g_one_ref[...] = one[:, :F]
    g_two_ref[...] = two_t[:classes]
    g_bias = one_t[F : F + 1]
    g_bias_ref[...] = g_bias
    square = jnp.where(feature, one * one + tiny_eps, 0.0)
    square_t = jnp.where(iota((LANES, hs), 0) < F, one_t * one_t + tiny_eps, 0.0)
    two_square = jnp.where(label, two * two + tiny_eps, 0.0)
    two_square_t = jnp.where(iota((LANES, hs), 0) < classes, two_t * two_t + tiny_eps, 0.0)
    col_new = keep_rate * col_ref[...] + new_rate * jnp.sum(square_t, axis=0, keepdims=True)
    row_new = keep_rate * row_ref[...] + new_rate * jnp.sum(two_square_t, axis=0, keepdims=True)
    second_new = keep_rate * second_ref[...] + new_rate * (g_bias * g_bias + tiny_eps)
    col_new_ref[...] = col_new
    row_new_ref[...] = row_new
    second_new_ref[...] = second_new
    step_one = one * lax.rsqrt(to_column(col_new, hs))
    step_one = jnp.where(feature, step_one, 0.0)
    step_one_ref[...] = step_one
    step_two_ref[...] = two_t * lax.rsqrt(row_new)
    step_two = jnp.where(label, two * lax.rsqrt(to_column(row_new, hs)), 0.0)
    step_bias = g_bias * lax.rsqrt(second_new)
    w_one = w_one_ref[...]
    w_two = w_two_ref[...]
    b_one = b_one_ref[...]
    lane = iota((1, LANES), 1)
    scalars = [
        total(row_new),
        total(w_one * w_one),
        total(w_two * w_two),
        total(b_one * b_one),
        total(step_bias * step_bias),
        stats_ref[0:1, HALF : HALF + 1],
    ]
    first = jnp.sum(square, axis=0, keepdims=True)
    for i, value in enumerate(scalars):
        first = jnp.where(lane == F + 1 + i, value, first)
    head = jnp.sum(step_two * step_two, axis=0, keepdims=True)
    sums = jnp.concatenate(
        [
            first,
            jnp.sum(step_one * step_one, axis=0, keepdims=True),
            jnp.sum(two_square, axis=0, keepdims=True) + pltpu.roll(jnp.broadcast_to(head, (8, LANES)), HALF, 1)[:1],
            jnp.where(lane < HALF, stats_ref[0:1], 0.0),
        ],
        axis=0,
    )
    sums_ref[...] = jnp.broadcast_to(sums[None], sums_ref.shape)


def update_kernel(
    sums_ref, step_one_ref, step_two_ref, g_bias_ref, second_new_ref,
    w_one_ref, b_one_ref, w_two_ref, b_two_ref, row_ref, col_ref, second_ref,
    loss_ref, w_one_new_ref, row_new_ref, w_two_new_ref, col_new_ref, b_one_new_ref,
    g_head_ref, b_two_new_ref, second_new_head_ref,
    *, hidden_units, slope_scale,
):
    classes = w_two_ref.shape[0]
    sums = jnp.sum(sums_ref[...], axis=0)
    row_total, one_total, two_total, bias_total, bias_rms, loss = [
        sums[0:1, F + 1 + i : F + 2 + i] for i in range(6)
    ]
    loss_ref[...] = loss * slope_scale
    row_new = keep_rate * row_ref[...] + new_rate * sums[0:1, :F]
    row_new_ref[...] = row_new
    col_new = keep_rate * col_ref[...] + new_rate * sums[2:3, :classes]
    col_new_ref[...] = col_new
    g_head = sums[3:4, :classes]
    g_head_ref[...] = g_head
    second = keep_rate * second_ref[...] + new_rate * (g_head * g_head + tiny_eps)
    second_new_head_ref[...] = second

    def clip(mean):
        return 1.0 / jnp.maximum(1.0, jnp.sqrt(mean) / clip_limit)

    def rate(mean):
        return step_rate * jnp.maximum(scale_eps, jnp.sqrt(mean))

    row_sum = jnp.sum(row_new, axis=1, keepdims=True)
    one_rms = jnp.sum(sums[1:2, :F] / row_new, axis=1, keepdims=True) * row_sum
    head_sums = pltpu.roll(jnp.broadcast_to(sums[2:3], (8, LANES)), HALF, 1)[:1, :classes]
    two_rms = jnp.sum(head_sums / col_new, axis=1, keepdims=True) * row_total
    one_rate = clip(one_rms / (F * hidden_units)) * rate(one_total / (F * hidden_units))
    step_one = step_one_ref[:, :F] * lax.rsqrt(row_new / row_sum)
    w_one_new_ref[...] = w_one_ref[...] - one_rate * step_one
    size = hidden_units * classes
    two_rate = clip(two_rms / size) * rate(two_total / size)
    scale = to_column(lax.rsqrt(col_new / row_total), classes)
    w_two_new_ref[...] = w_two_ref[...] - two_rate * (step_two_ref[:classes] * scale)
    bias_rate = clip(bias_rms / hidden_units) * rate(bias_total / hidden_units)
    b_one_new_ref[...] = b_one_ref[...] - bias_rate * (g_bias_ref[...] * lax.rsqrt(second_new_ref[...]))
    step_head = g_head * lax.rsqrt(second)
    b_two = b_two_ref[...]
    head_rate = clip(jnp.sum(step_head * step_head, axis=1, keepdims=True) / classes)
    head_rate = head_rate * rate(jnp.sum(b_two * b_two, axis=1, keepdims=True) / classes)
    b_two_new_ref[...] = b_two - head_rate * step_head


def local(
    features,
    neighbors,
    nbr_mask,
    send_rows,
    halo_count,
    pos_edges,
    neg_edges,
    w_one,
    b_one,
    w_two,
    b_two,
    w_one_row,
    w_one_col,
    w_two_row,
    w_two_col,
    b_one_second,
    b_two_second,
):
    peers = lax.axis_size("dom")
    ranks = lax.axis_size("rep")
    micros, rows, _ = features.shape
    classes = w_two.shape[1]
    hs = b_one.shape[0]
    slots = peers * HCAP
    total_edges = pos_edges.shape[1] * peers * micros * ranks

    x = jnp.transpose(features, (2, 0, 1))
    idx = jnp.transpose(neighbors, (0, 2, 1))
    mask = jnp.transpose(nbr_mask, (0, 2, 1))
    pos = jnp.transpose(pos_edges, (0, 2, 1))
    neg = jnp.transpose(neg_edges, (0, 2, 1))
    send = jnp.where(jnp.arange(HCAP) < halo_count[..., None], send_rows, -1)
    send = send.reshape(micros, 1, slots)
    slope_scale = 1.0 / (2.0 * total_edges)

    def exchange(sent):
        return lax.all_to_all(sent, "dom", 0, 0, tiled=True)

    turns = list(reversed(stages(peers)))
    weights = pack_shard(w_one, b_one, w_two)[None]
    weights = spread_stage(weights, *turns[0])
    table, sent = front(x, send)
    arrived_x = exchange(sent)
    sent_slot, sent_own, slot, own = select(idx, mask, table, send, pos, neg)
    sent = mean_sent(sent_slot, sent_own, table, arrived_x)
    arrived_agg = exchange(sent)
    for turn in turns[1:]:
        weights = spread_stage(weights, *turn)
    other = swap(weights)
    means = []
    for m in range(micros):
        means.append(mean_ends(slot, own, table, arrived_x, m, 2 * pos.shape[2]))
    head_bias = jnp.broadcast_to(jnp.pad(b_two, (0, LANES - classes)), (8, LANES))
    grad_mine, grad_other, stats = layers(
        means, pos, neg, arrived_agg, weights, other, head_bias, hs, rows, slope_scale
    )
    g = collect(grad_mine, grad_other)

    w_one_t = w_one.T
    w_two_t = w_two.T
    b_one_row = b_one[None]

    def out(*shape):
        return jax.ShapeDtypeStruct(shape, f32)

    vec = out(1, hs)
    count = peers * ranks
    g_one, g_two, g_bias, col_one, row_two, second_one, step_one, step_two, parts = pl.pallas_call(
        stats_kernel,
        out_shape=[
            out(hs, F), out(classes, hs), vec, vec, vec, vec,
            out(hs, LANES), out(LANES, hs), out(count, 4, LANES),
        ],
        name="stats",
    )(g, stats, w_one_t, b_one_row, w_two_t, w_one_col[None], w_two_row[None], b_one_second[None])
    parts = lax.all_to_all(parts, ("dom", "rep"), 0, 0, tiled=True)
    head = out(1, classes)
    loss, w_one_new, row_one, w_two_new, col_two, b_one_new, g_head, b_two_new, second_two = pl.pallas_call(
        lambda *refs: update_kernel(
            *refs, hidden_units=hs * count, slope_scale=slope_scale
        ),
        out_shape=[
            out(1, 1), out(hs, F), out(1, F), out(classes, hs), head, vec, head, head, head,
        ],
        name="update",
    )(
        parts, step_one, step_two, g_bias, second_one,
        w_one_t, b_one_row, w_two_t, b_two[None], w_one_row[None], w_two_col[None], b_two_second[None],
    )
    return (
        loss[0, 0],
        g_one.T,
        w_one_new.T,
        row_one[0],
        col_one[0],
        g_two.T,
        w_two_new.T,
        row_two[0],
        col_two[0],
        g_bias[0],
        b_one_new[0],
        second_one[0],
        g_head[0],
        b_two_new[0],
        second_two[0],
    )


def solution(mesh):
    return jax.shard_map(
        local,
        mesh=mesh,
        in_specs=(
            P("rep", "dom", None),
            P("rep", "dom", None),
            P("rep", "dom", None),
            P("rep", "dom", None),
            P("rep", "dom"),
            P("rep", "dom", None),
            P("rep", "dom", None),
            P(None, ("dom", "rep")),
            P(("dom", "rep")),
            P(("dom", "rep"), None),
            P(),
            P(),
            P(("dom", "rep")),
            P(("dom", "rep")),
            P(),
            P(("dom", "rep")),
            P(),
        ),
        out_specs=(
            P(),
            P(None, ("dom", "rep")),
            P(None, ("dom", "rep")),
            P(),
            P(("dom", "rep")),
            P(("dom", "rep"), None),
            P(("dom", "rep"), None),
            P(("dom", "rep")),
            P(),
            P(("dom", "rep")),
            P(("dom", "rep")),
            P(("dom", "rep")),
            P(),
            P(),
            P(),
        ),
        check_vma=False,
    )
```

```python
import jax
import jax.numpy as jnp
from jax import lax
from jax.experimental import pallas as pl
from jax.experimental.pallas import tpu as pltpu
from jax.sharding import PartitionSpec as P


F = 100
HCAP = 8
STEP = 20
LANES = 128
HALF = 64
GROUP = 16
HID_BLOCK = 512
COL_BLOCK = 2048

tiny_eps = 1e-30
scale_eps = 0.001
clip_limit = 1.0
step_rate = 0.3
keep_rate = 1.0 - STEP**-0.8
new_rate = STEP**-0.8
f32 = jnp.float32
bf16 = jnp.bfloat16


def dot(a, b, dims=((1,), (0,))):
    return lax.dot_general(a, b, (dims, ((), ())), preferred_element_type=f32)


def split(x):
    hi = x.astype(bf16)
    lo = (x - hi.astype(f32)).astype(bf16)
    return hi, lo


def iota(shape, dim):
    return lax.broadcasted_iota(jnp.int32, shape, dim)


def one_hot(cond):
    return jnp.where(cond, 1.0, 0.0).astype(bf16)


def picked(table, index, base=0):
    which = one_hot(iota((table.shape[1], index.shape[1]), 0) + base == index)
    both = dot(table, which)
    return both[:LANES] + both[LANES:]


def sent_rows(table, index, out_ref, micro):
    rows = picked(table, index).T
    out_ref[:, micro] = rows.reshape(out_ref.shape[0], HCAP, LANES)


def front_kernel(x_ref, send_ref, table_ref, out_ref, full):
    full[...] = jnp.where(iota(full.shape, 0) == F, 1.0, 0.0)
    for m in range(send_ref.shape[0]):
        full[:F] = x_ref[:, m, :]
        hi, lo = split(full[...])
        table_ref[m, :LANES] = hi
        table_ref[m, LANES:] = lo
        sent_rows(table_ref[m], send_ref[m], out_ref, m)


def front(x, send):
    _, micros, rows = x.shape
    peers = send.shape[2] // HCAP
    return pl.pallas_call(
        front_kernel,
        out_shape=[
            jax.ShapeDtypeStruct((micros, 2 * LANES, rows), bf16),
            jax.ShapeDtypeStruct((peers, micros, HCAP, LANES), f32),
        ],
        scratch_shapes=[pltpu.VMEM((LANES, rows), f32)],
        name="front",
    )(x, send)


def arrived_table(ref, micro, degree=None):
    slots = ref.shape[0] * HCAP
    rows = ref[:, micro].reshape(slots, LANES)
    if degree is not None:
        rows = jnp.where(iota(rows.shape, 1) == F, degree, rows)
    return jnp.concatenate(split(rows.T), axis=0)


def edge_row(pos_ref, neg_ref, micro, side):
    pos = pos_ref[micro, side : side + 1, :]
    return jnp.concatenate([pos, neg_ref[micro, side : side + 1, :]], axis=1)


def select_kernel(
    idx_ref, mask_ref, table_ref, send_ref, pos_ref, neg_ref,
    sent_slot_ref, sent_own_ref, slot_ref, own_ref, wide,
):
    degree = idx_ref.shape[1]
    for m in range(idx_ref.shape[0]):
        slot = jnp.where(mask_ref[m] > 0, idx_ref[m] + 1, 0)
        wide[:degree] = (slot >> 8).astype(f32).astype(bf16)
        wide[degree : 2 * degree] = (slot & 255).astype(f32).astype(bf16)
        wide[2 * degree :] = table_ref[m]
        count = 2 * pos_ref.shape[2]
        ends = [(edge_row(pos_ref, neg_ref, m, k), slot_ref, own_ref, k * count) for k in range(2)]
        for index, slots, owns, at in [(send_ref[m], sent_slot_ref, sent_own_ref, 0)] + ends:
            stop = at + index.shape[1]
            which = one_hot(iota((wide.shape[1], index.shape[1]), 0) == index)
            found = dot(wide[...], which)
            high = found[:degree].astype(jnp.int32)
            slots[m, :, at:stop] = high * 256 + found[degree : 2 * degree].astype(jnp.int32)
            own = found[2 * degree :]
            owns[m, :, at:stop] = own[:LANES] + own[LANES:]


def select(idx, mask, table, send, pos, neg):
    micros, degree, rows = idx.shape
    shapes = []
    for count in (send.shape[2], 4 * pos.shape[2]):
        shapes.append(jax.ShapeDtypeStruct((micros, degree, count), jnp.int32))
        shapes.append(jax.ShapeDtypeStruct((micros, LANES, count), f32))
    return pl.pallas_call(
        select_kernel,
        out_shape=shapes,
        scratch_shapes=[pltpu.VMEM((2 * degree + 2 * LANES, rows), bf16)],
        name="select",
    )(idx, mask, table, send, pos, neg)


def count_slots(slots, counts):
    degree, nodes = slots.shape
    width = degree * GROUP
    slots = slots - 1
    lane_part = iota((degree, width), 1) // GROUP
    row = iota((degree, width), 0)
    parts = []
    for at in range(0, nodes, width):
        size = min(width, nodes - at)
        piece = slots[:, at : at + size]
        if size < width:
            piece = jnp.concatenate([piece, jnp.full((degree, width - size), -1, jnp.int32)], axis=1)
        turned = piece
        for d in range(1, GROUP):
            moved = pltpu.roll(pltpu.roll(piece, d, 0), width - GROUP * d, 1)
            turned = jnp.where(lane_part == ((row - d) & (GROUP - 1)), moved, turned)
        parts.append(turned)
    turned = jnp.concatenate(parts, axis=0)
    same = (iota((GROUP, width), 1) & (GROUP - 1)) == iota((GROUP, width), 0)
    same = one_hot(same)
    none = jnp.zeros((GROUP, width), bf16)
    forms = []
    for span in (LANES, 2 * LANES):
        high_part = (turned >> (span.bit_length() - 1)).astype(f32)
        low_part = (turned & (span - 1)).astype(f32)
        low_rows = iota((span, width), 0).astype(f32).astype(bf16)
        forms.append((span, high_part, low_part, low_rows))
    for g in range(nodes // GROUP):
        span, high_part, low_part, low_rows = forms[g & 1]
        high = -(-counts.shape[1] // span)
        hi = jnp.broadcast_to(high_part[g : g + 1], (GROUP, width)).astype(bf16)
        lo = jnp.broadcast_to(low_part[g : g + 1], (span, width)).astype(bf16)
        left = jnp.concatenate([jnp.where(hi == h, same, none) for h in range(high)], axis=0)
        right = jnp.where(low_rows == lo, jnp.ones((span, width), bf16), jnp.zeros((span, width), bf16))
        found = dot(left, right, ((1,), (1,))).astype(bf16)
        for h in range(high):
            at = h * span
            size = min(span, counts.shape[1] - at)
            counts[g * GROUP : (g + 1) * GROUP, at : at + size] = found[
                h * GROUP : (h + 1) * GROUP, :size
            ]


def mean_columns(slots, own, table, arrived, counts):
    count_slots(slots, counts)
    rows = table.shape[1]
    both = dot(table, counts[:, :rows], ((1,), (1,)))
    both = both + dot(arrived, counts[:, rows:], ((1,), (1,)))
    total = both[:LANES] + both[LANES:] + own
    degree = total[F : F + 1]
    mean = jnp.where(degree > 0.5, total / jnp.maximum(degree, 1.0), 0.0)
    return jnp.where(iota(mean.shape, 0) == F, jnp.minimum(degree, 1.0), mean)


def mean_sent_kernel(slot_ref, own_ref, table_ref, arrived_ref, out_ref, counts):
    for m in range(slot_ref.shape[0]):
        arrived = arrived_table(arrived_ref, m, 1.0)
        mean = mean_columns(slot_ref[m], own_ref[m], table_ref[m], arrived, counts)
        out_ref[:, m] = mean.T.reshape(out_ref.shape[0], HCAP, LANES)


def mean_sent(slot, own, table, arrived):
    micros, degree, _ = slot.shape
    sent = arrived.shape[0] * HCAP
    rows = table.shape[2]
    return pl.pallas_call(
        mean_sent_kernel,
        grid=(1,),
        in_specs=[
            pl.BlockSpec((micros, degree, sent), lambda i: (0, 0, 0)),
            pl.BlockSpec((micros, LANES, sent), lambda i: (0, 0, 0)),
            pl.BlockSpec(table.shape, lambda i: (0, 0, 0)),
            pl.BlockSpec(arrived.shape, lambda i: (0, 0, 0, 0)),
        ],
        out_specs=pl.BlockSpec(arrived.shape, lambda i: (0, 0, 0, 0)),
        out_shape=jax.ShapeDtypeStruct(arrived.shape, f32),
        scratch_shapes=[pltpu.VMEM((sent, rows + sent), bf16)],
        name="mean_sent",
    )(slot, own, table, arrived)


def mean_ends_kernel(slot_ref, own_ref, table_ref, arrived_ref, out_ref, counts):
    arrived = arrived_table(arrived_ref, 0, 1.0)
    out_ref[...] = mean_columns(slot_ref[0], own_ref[0], table_ref[0], arrived, counts)


def mean_ends(slot, own, table, arrived, micro, block):
    degree = slot.shape[1]
    peers = arrived.shape[0]
    sent = peers * HCAP
    rows = table.shape[2]
    count = slot.shape[2]
    return pl.pallas_call(
        mean_ends_kernel,
        grid=(count // block,),
        in_specs=[
            pl.BlockSpec((1, degree, block), lambda b: (micro, 0, b)),
            pl.BlockSpec((1, LANES, block), lambda b: (micro, 0, b)),
            pl.BlockSpec((1, 2 * LANES, rows), lambda b: (micro, 0, 0)),
            pl.BlockSpec((peers, 1, HCAP, LANES), lambda b: (0, micro, 0, 0)),
        ],
        out_specs=pl.BlockSpec((LANES, block), lambda b: (0, b)),
        out_shape=jax.ShapeDtypeStruct((LANES, count), f32),
        scratch_shapes=[pltpu.VMEM((block, rows + sent), bf16)],
        name="mean_ends",
    )(slot, own, table, arrived)


def first_block(ref, start, shards, hs):
    return ref[pl.ds(start, shards), 0:hs, :].reshape(shards * hs, LANES)


def head_block(ref, start, shards, hs):
    if hs % GROUP:
        return ref[pl.ds(start, shards), hs : 2 * hs, :].reshape(shards * hs, LANES)
    half = hs // 2
    packed = ref[pl.ds(start, shards), hs : hs + half, :].reshape(shards * half, LANES)
    low = iota(packed.shape, 1) < HALF
    left = jnp.where(low, packed, 0.0).reshape(shards, half, LANES)
    right = jnp.where(low, pltpu.roll(packed, HALF, 1), 0.0).reshape(shards, half, LANES)
    return jnp.concatenate([left, right], axis=1).reshape(shards * hs, LANES)


def head_terms(block):
    hi = block.astype(bf16)
    rest = block - hi.astype(f32)
    return hi, (hi.astype(f32) + pltpu.roll(rest, HALF, 1)).astype(bf16)


def layers_kernel(
    *refs, hs, nodes, slope_scale,
):
    agg_row, agg_col, hidden, out_col, dz_col, dz_row = refs[-6:]
    grad_mine_ref, grad_other_ref, stats_ref = refs[-9:-6]
    pos_ref, neg_ref, arrived_ref, mine_ref, other_ref, head_bias_ref = refs[-15:-9]
    parts = refs[:-15]
    micros, sides, count = pos_ref.shape[0], 2, 2 * pos_ref.shape[2]
    ends = micros * sides * count
    shards = HID_BLOCK // hs
    blocks = mine_ref.shape[0] // shards

    for m in range(micros):
        far = picked(arrived_table(arrived_ref, m), edge_row(pos_ref, neg_ref, m, 1), nodes)
        for s in range(sides):
            at = (m * sides + s) * count
            cols = parts[m][:, s * count : (s + 1) * count]
            if s == 1:
                cols = cols + far
            hi, lo = split(cols)
            agg_col[:LANES, at : at + count] = hi
            agg_col[LANES:, at : at + count] = lo
            hi, lo = split(cols.T)
            agg_row[at : at + count, :LANES] = hi
            agg_row[at : at + count, LANES:] = lo

    out_col[...] = jnp.zeros(out_col.shape, f32)

    for side, ref in enumerate((mine_ref, other_ref)):

        def forward(c, carry, ref=ref, side=side):
            first = first_block(ref, c * shards, shards, hs)
            hi, lo = split(first)
            both = jnp.concatenate([hi, lo], axis=1)
            head_hi, head_both = head_terms(head_block(ref, c * shards, shards, hs))
            head = jnp.concatenate([head_both, head_hi], axis=0)
            slot = side * blocks + c
            for n in range(0, ends, COL_BLOCK):
                cols = slice(n, n + COL_BLOCK)
                upper = agg_col[:LANES, cols]
                pre = dot(both, jnp.concatenate([upper, upper], axis=0))
                pre = pre + dot(hi, agg_col[LANES:, cols])
                act_hi, act_lo = split(jnp.maximum(pre, 0.0))
                hidden[slot, :HID_BLOCK, cols] = act_hi
                hidden[slot, HID_BLOCK:, cols] = act_lo
                act = jnp.concatenate([act_hi, act_lo], axis=0)
                out_col[:, cols] += dot(head, act, ((0,), (0,)))
            return carry

        lax.fori_loop(0, blocks, forward, 0)

    bias = to_column(head_bias_ref[...], HALF)
    loss = jnp.zeros((1, 1), f32)
    head_grad = jnp.zeros((HALF, 1), f32)
    sign = jnp.where(iota((1, count), 1) < count // 2, -1.0, 1.0)
    for m in range(micros):
        at = m * sides * count
        mid = at + count
        end = mid + count
        z_u = out_col[:HALF, at:mid] + out_col[HALF:, at:mid] + bias
        z_v = out_col[:HALF, mid:end] + out_col[HALF:, mid:end] + bias
        score = jnp.sum(z_u * z_v, axis=0, keepdims=True) * sign
        tail = jnp.exp(-jnp.abs(score))
        plus = jnp.maximum(score, 0.0) + jnp.log1p(tail)
        loss = loss + jnp.sum(plus, axis=1, keepdims=True)
        slope = sign * jax.nn.sigmoid(score) * slope_scale
        for start, grad in ((at, slope * z_v), (mid, slope * z_u)):
            stop = start + count
            head_grad = head_grad + jnp.sum(grad, axis=1, keepdims=True)
            hi, lo = split(grad)
            dz_col[:HALF, start:stop] = hi
            dz_col[HALF : 2 * HALF, start:stop] = hi
            dz_col[2 * HALF : 3 * HALF, start:stop] = lo
            dz_col[3 * HALF :, start:stop] = jnp.zeros((HALF, count), bf16)
            both = jnp.concatenate([hi.astype(f32), lo.astype(f32)], axis=0)
            dz_row[start:stop] = both.T.astype(bf16)
    wide = jnp.broadcast_to(head_grad, (HALF, LANES))
    wide = jnp.concatenate([wide, jnp.broadcast_to(loss, (HALF, LANES))], axis=0)
    stats_ref[...] = wide.T[:8]

    for side, (ref, grad_ref) in enumerate(((mine_ref, grad_mine_ref), (other_ref, grad_other_ref))):

        def backward(c, carry, ref=ref, grad_ref=grad_ref, side=side):
            head_hi, head_both = head_terms(head_block(ref, c * shards, shards, hs))
            head = jnp.concatenate([head_both, head_hi], axis=1)
            slot = side * blocks + c
            head_sum = jnp.zeros((HID_BLOCK, LANES), f32)
            first_sum = jnp.zeros((HID_BLOCK, LANES), f32)
            for n in range(0, ends, COL_BLOCK):
                cols = slice(n, n + COL_BLOCK)
                act_hi = hidden[slot, :HID_BLOCK, cols]
                act_lo = hidden[slot, HID_BLOCK:, cols]
                grad = dot(head, dz_col[:, cols])
                grad = jnp.where(act_hi.astype(f32) > 0.0, grad, 0.0)
                hi, lo = split(grad)
                head_sum = head_sum + dot(act_hi, dz_row[cols]) + dot(act_lo, dz_row[cols])
                both = dot(hi, agg_row[cols])
                first_sum = first_sum + both[:, :LANES] + both[:, LANES:]
                first_sum = first_sum + dot(lo, agg_row[cols, :LANES])
            grad_ref[pl.ds(c * shards, shards), 0:hs, :] = first_sum.reshape(shards, hs, LANES)
            folded = (head_sum + pltpu.roll(head_sum, HALF, 1)).reshape(shards, hs, LANES)
            if hs % GROUP:
                grad_ref[pl.ds(c * shards, shards), hs : 2 * hs, :] = folded
            else:
                half = hs // 2
                low = iota((shards, half, LANES), 2) < HALF
                grad_ref[pl.ds(c * shards, shards), hs : hs + half, :] = jnp.where(
                    low, folded[:, :half], folded[:, half:]
                )
            return carry

        lax.fori_loop(0, blocks, backward, 0)


def layers(parts, pos, neg, arrived, mine, other, head_bias, hs, nodes, slope_scale):
    ends = len(parts) * parts[0].shape[1]
    blocks = 2 * mine.shape[0] * hs // HID_BLOCK
    shape = jax.ShapeDtypeStruct(mine.shape, f32)
    return pl.pallas_call(
        lambda *refs: layers_kernel(*refs, hs=hs, nodes=nodes, slope_scale=slope_scale),
        out_shape=[shape, shape, jax.ShapeDtypeStruct((8, LANES), f32)],
        scratch_shapes=[
            pltpu.VMEM((ends, 2 * LANES), bf16),
            pltpu.VMEM((2 * LANES, ends), bf16),
            pltpu.VMEM((blocks, 2 * HID_BLOCK, ends), bf16),
            pltpu.VMEM((LANES, ends), f32),
            pltpu.VMEM((4 * HALF, ends), bf16),
            pltpu.VMEM((ends, LANES), bf16),
        ],
        name="layers",
    )(*parts, pos, neg, arrived, mine, other, head_bias)


def stages(size):
    found = []
    stride = 1
    while stride < size:
        radix = min(4, size // stride)
        found.append((stride, radix))
        stride *= radix
    return found


def trade(x, offset):
    size = lax.axis_size("dom")
    return lax.ppermute(x, "dom", [(i, i ^ offset) for i in range(size)])


def swap(x):
    return lax.ppermute(x, "rep", [(0, 1), (1, 0)])


def spread_stage(x, stride, radix):
    return jnp.concatenate([x] + [trade(x, stride * k) for k in range(1, radix)], axis=0)


def collect(mine, other):
    x = mine + swap(other)
    for stride, radix in stages(lax.axis_size("dom")):
        parts = x.reshape((radix, x.shape[0] // radix) + x.shape[1:])
        y = parts[0]
        for k in range(1, radix):
            y = y + trade(parts[k], stride * k)
        x = y
    return x[0]


def pack_shard(w_one, b_one, w_two):
    hs = b_one.shape[0]
    first = jnp.concatenate([w_one.T, b_one[:, None]], axis=1)
    first = jnp.pad(first, ((0, 0), (0, LANES - first.shape[1])))
    if hs % GROUP:
        head = jnp.pad(w_two, ((0, 0), (0, LANES - w_two.shape[1])))
    else:
        head = jnp.pad(w_two, ((0, 0), (0, HALF - w_two.shape[1])))
        head = jnp.concatenate([head[: hs // 2], head[hs // 2 :]], axis=1)
    return jnp.concatenate([first, head], axis=0)


def unpack_head(g, hs):
    head = g[hs:]
    if hs % GROUP:
        return head
    low = iota((hs // 2, LANES), 1) < HALF
    right = jnp.where(low, pltpu.roll(head, HALF, 1), 0.0)
    return jnp.concatenate([jnp.where(low, head, 0.0), right], axis=0)


def to_column(row, hs):
    wide = jnp.broadcast_to(row, (8, row.shape[1]))
    if row.shape[1] < LANES:
        wide = jnp.concatenate([wide, jnp.zeros((8, LANES - row.shape[1]), f32)], axis=1)
    return wide.T[:hs, :1]


def total(x):
    return jnp.sum(jnp.sum(x, axis=1, keepdims=True), axis=0, keepdims=True)


def stats_kernel(
    g_ref, stats_ref, w_one_ref, b_one_ref, w_two_ref, col_ref, row_ref, second_ref,
    g_one_ref, g_two_ref, g_bias_ref, col_new_ref, row_new_ref, second_new_ref,
    step_one_ref, step_two_ref, sums_ref,
):
    hs = b_one_ref.shape[1]
    classes = w_two_ref.shape[0]
    g = g_ref[...]
    one = g[:hs]
    one_t = one.T
    two = unpack_head(g, hs)
    two_t = two.T
    feature = iota((hs, LANES), 1) < F
    label = iota((hs, LANES), 1) < classes
    g_one_ref[...] = one[:, :F]
    g_two_ref[...] = two_t[:classes]
    g_bias = one_t[F : F + 1]
    g_bias_ref[...] = g_bias
    square = jnp.where(feature, one * one + tiny_eps, 0.0)
    square_t = jnp.where(iota((LANES, hs), 0) < F, one_t * one_t + tiny_eps, 0.0)
    two_square = jnp.where(label, two * two + tiny_eps, 0.0)
    two_square_t = jnp.where(iota((LANES, hs), 0) < classes, two_t * two_t + tiny_eps, 0.0)
    col_new = keep_rate * col_ref[...] + new_rate * jnp.sum(square_t, axis=0, keepdims=True)
    row_new = keep_rate * row_ref[...] + new_rate * jnp.sum(two_square_t, axis=0, keepdims=True)
    second_new = keep_rate * second_ref[...] + new_rate * (g_bias * g_bias + tiny_eps)
    col_new_ref[...] = col_new
    row_new_ref[...] = row_new
    second_new_ref[...] = second_new
    step_one = one * lax.rsqrt(to_column(col_new, hs))
    step_one = jnp.where(feature, step_one, 0.0)
    step_one_ref[...] = step_one
    step_two_ref[...] = two_t * lax.rsqrt(row_new)
    step_two = jnp.where(label, two * lax.rsqrt(to_column(row_new, hs)), 0.0)
    step_bias = g_bias * lax.rsqrt(second_new)
    w_one = w_one_ref[...]
    w_two = w_two_ref[...]
    b_one = b_one_ref[...]
    lane = iota((1, LANES), 1)
    scalars = [
        total(row_new),
        total(w_one * w_one),
        total(w_two * w_two),
        total(b_one * b_one),
        total(step_bias * step_bias),
        stats_ref[0:1, HALF : HALF + 1],
    ]
    first = jnp.sum(square, axis=0, keepdims=True)
    for i, value in enumerate(scalars):
        first = jnp.where(lane == F + 1 + i, value, first)
    head = jnp.sum(step_two * step_two, axis=0, keepdims=True)
    sums = jnp.concatenate(
        [
            first,
            jnp.sum(step_one * step_one, axis=0, keepdims=True),
            jnp.sum(two_square, axis=0, keepdims=True) + pltpu.roll(jnp.broadcast_to(head, (8, LANES)), HALF, 1)[:1],
            jnp.where(lane < HALF, stats_ref[0:1], 0.0),
        ],
        axis=0,
    )
    sums_ref[...] = jnp.broadcast_to(sums[None], sums_ref.shape)


def update_kernel(
    sums_ref, step_one_ref, step_two_ref, g_bias_ref, second_new_ref,
    w_one_ref, b_one_ref, w_two_ref, b_two_ref, row_ref, col_ref, second_ref,
    loss_ref, w_one_new_ref, row_new_ref, w_two_new_ref, col_new_ref, b_one_new_ref,
    g_head_ref, b_two_new_ref, second_new_head_ref,
    *, hidden_units, slope_scale,
):
    classes = w_two_ref.shape[0]
    sums = jnp.sum(sums_ref[...], axis=0)
    row_total, one_total, two_total, bias_total, bias_rms, loss = [
        sums[0:1, F + 1 + i : F + 2 + i] for i in range(6)
    ]
    loss_ref[...] = loss * slope_scale
    row_new = keep_rate * row_ref[...] + new_rate * sums[0:1, :F]
    row_new_ref[...] = row_new
    col_new = keep_rate * col_ref[...] + new_rate * sums[2:3, :classes]
    col_new_ref[...] = col_new
    g_head = sums[3:4, :classes]
    g_head_ref[...] = g_head
    second = keep_rate * second_ref[...] + new_rate * (g_head * g_head + tiny_eps)
    second_new_head_ref[...] = second

    def clip(mean):
        return 1.0 / jnp.maximum(1.0, jnp.sqrt(mean) / clip_limit)

    def rate(mean):
        return step_rate * jnp.maximum(scale_eps, jnp.sqrt(mean))

    row_sum = jnp.sum(row_new, axis=1, keepdims=True)
    one_rms = jnp.sum(sums[1:2, :F] / row_new, axis=1, keepdims=True) * row_sum
    head_sums = pltpu.roll(jnp.broadcast_to(sums[2:3], (8, LANES)), HALF, 1)[:1, :classes]
    two_rms = jnp.sum(head_sums / col_new, axis=1, keepdims=True) * row_total
    one_rate = clip(one_rms / (F * hidden_units)) * rate(one_total / (F * hidden_units))
    step_one = step_one_ref[:, :F] * lax.rsqrt(row_new / row_sum)
    w_one_new_ref[...] = w_one_ref[...] - one_rate * step_one
    size = hidden_units * classes
    two_rate = clip(two_rms / size) * rate(two_total / size)
    scale = to_column(lax.rsqrt(col_new / row_total), classes)
    w_two_new_ref[...] = w_two_ref[...] - two_rate * (step_two_ref[:classes] * scale)
    bias_rate = clip(bias_rms / hidden_units) * rate(bias_total / hidden_units)
    b_one_new_ref[...] = b_one_ref[...] - bias_rate * (g_bias_ref[...] * lax.rsqrt(second_new_ref[...]))
    step_head = g_head * lax.rsqrt(second)
    b_two = b_two_ref[...]
    head_rate = clip(jnp.sum(step_head * step_head, axis=1, keepdims=True) / classes)
    head_rate = head_rate * rate(jnp.sum(b_two * b_two, axis=1, keepdims=True) / classes)
    b_two_new_ref[...] = b_two - head_rate * step_head


def local(
    features,
    neighbors,
    nbr_mask,
    send_rows,
    halo_count,
    pos_edges,
    neg_edges,
    w_one,
    b_one,
    w_two,
    b_two,
    w_one_row,
    w_one_col,
    w_two_row,
    w_two_col,
    b_one_second,
    b_two_second,
):
    peers = lax.axis_size("dom")
    ranks = lax.axis_size("rep")
    micros, rows, _ = features.shape
    classes = w_two.shape[1]
    hs = b_one.shape[0]
    slots = peers * HCAP
    total_edges = pos_edges.shape[1] * peers * micros * ranks

    x = jnp.transpose(features, (2, 0, 1))
    idx = jnp.transpose(neighbors, (0, 2, 1))
    mask = jnp.transpose(nbr_mask, (0, 2, 1))
    pos = jnp.transpose(pos_edges, (0, 2, 1))
    neg = jnp.transpose(neg_edges, (0, 2, 1))
    send = jnp.where(jnp.arange(HCAP) < halo_count[..., None], send_rows, -1)
    send = send.reshape(micros, 1, slots)
    slope_scale = 1.0 / (2.0 * total_edges)

    def exchange(sent):
        return lax.all_to_all(sent, "dom", 0, 0, tiled=True)

    turns = list(reversed(stages(peers)))
    weights = pack_shard(w_one, b_one, w_two)[None]
    weights = spread_stage(weights, *turns[0])
    table, sent = front(x, send)
    arrived_x = exchange(sent)
    sent_slot, sent_own, slot, own = select(idx, mask, table, send, pos, neg)
    sent = mean_sent(sent_slot, sent_own, table, arrived_x)
    arrived_agg = exchange(sent)
    for turn in turns[1:]:
        weights = spread_stage(weights, *turn)
    other = swap(weights)
    means = []
    for m in range(micros):
        means.append(mean_ends(slot, own, table, arrived_x, m, 2 * pos.shape[2]))
    head_bias = b_two[None]
    grad_mine, grad_other, stats = layers(
        means, pos, neg, arrived_agg, weights, other, head_bias, hs, rows, slope_scale
    )
    g = collect(grad_mine, grad_other)

    w_one_t = w_one.T
    w_two_t = w_two.T
    b_one_row = b_one[None]

    def out(*shape):
        return jax.ShapeDtypeStruct(shape, f32)

    vec = out(1, hs)
    count = peers * ranks
    g_one, g_two, g_bias, col_one, row_two, second_one, step_one, step_two, parts = pl.pallas_call(
        stats_kernel,
        out_shape=[
            out(hs, F), out(classes, hs), vec, vec, vec, vec,
            out(hs, LANES), out(LANES, hs), out(count, 4, LANES),
        ],
        name="stats",
    )(g, stats, w_one_t, b_one_row, w_two_t, w_one_col[None], w_two_row[None], b_one_second[None])
    parts = lax.all_to_all(parts, ("dom", "rep"), 0, 0, tiled=True)
    head = out(1, classes)
    loss, w_one_new, row_one, w_two_new, col_two, b_one_new, g_head, b_two_new, second_two = pl.pallas_call(
        lambda *refs: update_kernel(
            *refs, hidden_units=hs * count, slope_scale=slope_scale
        ),
        out_shape=[
            out(1, 1), out(hs, F), out(1, F), out(classes, hs), head, vec, head, head, head,
        ],
        name="update",
    )(
        parts, step_one, step_two, g_bias, second_one,
        w_one_t, b_one_row, w_two_t, b_two[None], w_one_row[None], w_two_col[None], b_two_second[None],
    )
    return (
        loss[0, 0],
        g_one.T,
        w_one_new.T,
        row_one[0],
        col_one[0],
        g_two.T,
        w_two_new.T,
        row_two[0],
        col_two[0],
        g_bias[0],
        b_one_new[0],
        second_one[0],
        g_head[0],
        b_two_new[0],
        second_two[0],
    )


def solution(mesh):
    return jax.shard_map(
        local,
        mesh=mesh,
        in_specs=(
            P("rep", "dom", None),
            P("rep", "dom", None),
            P("rep", "dom", None),
            P("rep", "dom", None),
            P("rep", "dom"),
            P("rep", "dom", None),
            P("rep", "dom", None),
            P(None, ("dom", "rep")),
            P(("dom", "rep")),
            P(("dom", "rep"), None),
            P(),
            P(),
            P(("dom", "rep")),
            P(("dom", "rep")),
            P(),
            P(("dom", "rep")),
            P(),
        ),
        out_specs=(
            P(),
            P(None, ("dom", "rep")),
            P(None, ("dom", "rep")),
            P(),
            P(("dom", "rep")),
            P(("dom", "rep"), None),
            P(("dom", "rep"), None),
            P(("dom", "rep")),
            P(),
            P(("dom", "rep")),
            P(("dom", "rep")),
            P(("dom", "rep")),
            P(),
            P(),
            P(),
        ),
        check_vma=False,
    )
```
